256 devices in a mesh: nodes: 128 (over x, y, z), mp: 2 (over core).
Axes of the slice: x: 4, y: 4, z: 8, core: 2. Of those that a mesh axis runs over, the one named last changes fastest.
Arguments:
- memory: bfloat16 [262144, 512], P('nodes'), may hold values from -6 to 6
- ev_time: int32 [16384], P('nodes'), may hold values from 0 to 1023
- nbr_time: int32 [16384, 2, 16], P('nodes'), may hold values from 0 to 1023
- edge_feat: bfloat16 [16384, 128], P('nodes', 'mp'), may hold values from -6 to 6
- self_slot: int32 [16384, 2], P('nodes'), may hold values from 0 to 511
- nbr_slot: int32 [16384, 2, 16], P('nodes'), may hold values from 0 to 4095
- serve_self: int32 [128, 128, 4], P('nodes'), may hold values from 0 to 2047
- serve_rows: int32 [128, 128, 32], P('nodes'), may hold values from 0 to 2047
- freq: float32 [128], replicated, may hold values from 0.001 to 0.5
- phase: float32 [128], replicated, may hold values from -3.140625 to 3.140625
- w_query: bfloat16 [640, 512], P(None, 'mp'), may hold values from -0.25 to 0.25
- w_key: bfloat16 [640, 512], P(None, 'mp'), may hold values from -0.25 to 0.25
- w_value: bfloat16 [640, 512], P(None, 'mp'), may hold values from -0.25 to 0.25
- w_out: bfloat16 [512, 512], P('mp'), may hold values from -0.25 to 0.25
- w_self: bfloat16 [512, 512], P('mp'), may hold values from -0.25 to 0.25
- w_msg_self: bfloat16 [512, 512], P('mp'), may hold values from -0.25 to 0.25
- w_msg_other: bfloat16 [512, 512], P('mp'), may hold values from -0.25 to 0.25
- w_msg_time: bfloat16 [128, 512], P('mp'), may hold values from -0.5 to 0.5
- w_msg_edge: bfloat16 [128, 512], P('mp'), may hold values from -0.5 to 0.5
- w_in: bfloat16 [512, 3, 512], P(None, None, 'mp'), may hold values from -0.25 to 0.25
- w_hid: bfloat16 [512, 3, 512], P(None, None, 'mp'), may hold values from -0.25 to 0.25
Outputs:
- embedding: bfloat16 [16384, 2, 512], P('nodes')
- memory_out: bfloat16 [262144, 512], P('nodes', 'mp')
The draws below stay inside these ranges and needn't reach their ends.
Inputs may be any that keep to these rules, and one draw needn't show every extreme that they name: `self_slot`: slot index o * 4 + s refers to endpoint slot s of owner o. `nbr_slot`: slot index o * 32 + s refers to neighbour slot s of owner o.
All inputs are finite; a program needn't handle non-finite values.
Results may differ from the reference program's by a relative error of at most 0.0075.
Values may be sent and summed in bfloat16 or wider, within the bound.
A program may use at most 128 MiB of HBM per device.

```python
import math
import jax
import jax.numpy as jnp
from jax import lax

W = 512
HEADS = 8
HEAD = 64
K = 16
TD = 128
EF = 128
MSG = 512
BINS = 1024
EV_DEV = 128
ROWS_DEV = 2048
CAP = 32
CAP_SELF = 4
PEERS = 128
EVENTS = 16384
NODES = 262144


def place_ends(result, own_key, smallest, largest):
    index_at = [jax.random.randint(jax.random.fold_in(own_key, axis), (), 0, length) for axis, length in enumerate(result.shape)]
    longest = result.shape.index(max(result.shape))
    neighbour = index_at[:longest] + [(index_at[longest] + 1) % result.shape[longest]] + index_at[longest + 1:]
    return result.at[tuple(index_at)].set(smallest).at[tuple(neighbour)].set(largest)


def steps_of(stream_key, extent, split, smallest, high):
    def one(dim, blocks):
        heights = jax.random.uniform(jax.random.fold_in(jax.random.fold_in(stream_key, 6), dim), (blocks,), jnp.float32, smallest / len(split), high / len(split))
        return jnp.repeat(jnp.exp(heights), extent[dim] // blocks).reshape((-1,) + (1,) * (len(extent) - dim - 1))

    gain = one(*split[0])
    for cut in split[1:]:
        gain = gain * one(*cut)
    return gain


def gaussian(key, shape, scale, reach, shards=(), kind=jnp.bfloat16):
    result = scale * jax.random.normal(key, shape, jnp.float32)
    if shards:
        result = result * steps_of(key, shape, shards, -0.22, 0.18)
    return jnp.clip(result, -reach, reach).astype(kind)


def setup_inputs(seed: int = 0) -> dict:
    splits = jax.random.split(jax.random.key(seed), 22)
    return {
        "memory": gaussian(splits[0], (NODES, W), 1.0, 6.0, ((0, 128),)),
        "ev_time": place_ends(jax.random.randint(splits[1], (EVENTS,), 0, BINS), jax.random.fold_in(splits[1], 1), 0, BINS - 1).astype(jnp.int32),
        "nbr_time": place_ends(jax.random.randint(splits[2], (EVENTS, 2, K), 0, BINS), jax.random.fold_in(splits[2], 1), 0, BINS - 1).astype(jnp.int32),
        "edge_feat": gaussian(splits[3], (EVENTS, EF), 1.0, 6.0, ((0, 128), (1, 2))),
        "self_slot": place_ends(jax.random.randint(splits[4], (EVENTS, 2), 0, PEERS * CAP_SELF), jax.random.fold_in(splits[4], 1), 0, (PEERS * CAP_SELF) - 1).astype(jnp.int32),
        "nbr_slot": place_ends(jax.random.randint(splits[5], (EVENTS, 2, K), 0, PEERS * CAP), jax.random.fold_in(splits[5], 1), 0, (PEERS * CAP) - 1).astype(jnp.int32),
        "serve_self": place_ends(jax.random.randint(splits[6], (PEERS, PEERS, CAP_SELF), 0, ROWS_DEV), jax.random.fold_in(splits[6], 1), 0, ROWS_DEV - 1).astype(jnp.int32),
        "serve_rows": place_ends(jax.random.randint(splits[7], (PEERS, PEERS, CAP), 0, ROWS_DEV), jax.random.fold_in(splits[7], 1), 0, ROWS_DEV - 1).astype(jnp.int32),
        "freq": jnp.clip(jnp.exp(jax.random.uniform(splits[8], (TD,), jnp.float32, math.log(0.001), math.log(0.5))), 0.001, 0.5),
        "phase": jnp.clip(jax.random.uniform(splits[9], (TD,), jnp.float32, -3.140625, 3.140625), -3.140625, 3.140625),
        "w_query": gaussian(splits[10], (W + TD, W), (W + TD) ** -0.5, 0.25, ((1, 2),)),
        "w_key": gaussian(splits[11], (W + TD, W), (W + TD) ** -0.5, 0.25, ((1, 2),)),
        "w_value": gaussian(splits[12], (W + TD, W), (W + TD) ** -0.5, 0.25, ((1, 2),)),
        "w_out": gaussian(splits[13], (W, W), W ** -0.5, 0.25, ((0, 2),)),
        "w_self": gaussian(splits[14], (W, W), W ** -0.5, 0.25, ((0, 2),)),
        "w_msg_self": gaussian(splits[15], (W, MSG), W ** -0.5, 0.25, ((0, 2),)),
        "w_msg_other": gaussian(splits[16], (W, MSG), W ** -0.5, 0.25, ((0, 2),)),
        "w_msg_time": gaussian(splits[17], (TD, MSG), TD ** -0.5, 0.5, ((0, 2),)),
        "w_msg_edge": gaussian(splits[18], (EF, MSG), EF ** -0.5, 0.5, ((0, 2),)),
        "w_in": gaussian(splits[19], (MSG, 3, W), MSG ** -0.5, 0.25, ((2, 2),)),
        "w_hid": gaussian(splits[20], (W, 3, W), W ** -0.5, 0.25, ((2, 2),)),
    }


def encode(delta, freq, phase):
    return jnp.cos(delta.astype(jnp.float32)[..., None] * freq + phase)

def reference(memory, ev_time, nbr_time, edge_feat, self_slot, nbr_slot, serve_self, serve_rows, freq, phase, w_query, w_key, w_value, w_out, w_self, w_msg_self, w_msg_other, w_msg_time, w_msg_edge, w_in, w_hid):
    owner_base = (jnp.arange(PEERS, dtype=jnp.int32) * ROWS_DEV)[:, None, None]
    nbr_table = jnp.transpose(owner_base + serve_rows.astype(jnp.int32), (1, 0, 2)).reshape(PEERS, PEERS * CAP)
    self_table = jnp.transpose(owner_base + serve_self.astype(jnp.int32), (1, 0, 2)).reshape(PEERS, PEERS * CAP_SELF)
    te_self = jnp.cos(phase).astype(jnp.bfloat16)[None]

    def block(args):
        self_look, nbr_look, times, nbr_times, edges, ntab, stab = args
        self_rows = stab[self_look]
        nbr_rows = ntab[nbr_look]
        self_mem = memory[self_rows].reshape(-1, W)
        nbrs = memory[nbr_rows].reshape(-1, W)
        other = memory[self_rows[:, ::-1]].reshape(-1, W)
        te_nbr = encode(times[:, None, None] - nbr_times, freq, phase).astype(jnp.bfloat16).reshape(-1, TD)
        query = (jnp.dot(self_mem, w_query[:W], preferred_element_type=jnp.float32) + jnp.dot(te_self, w_query[W:], preferred_element_type=jnp.float32)).astype(jnp.bfloat16)
        keys = (jnp.dot(nbrs, w_key[:W], preferred_element_type=jnp.float32) + jnp.dot(te_nbr, w_key[W:], preferred_element_type=jnp.float32)).astype(jnp.bfloat16)
        values = (jnp.dot(nbrs, w_value[:W], preferred_element_type=jnp.float32) + jnp.dot(te_nbr, w_value[W:], preferred_element_type=jnp.float32)).astype(jnp.bfloat16)
        qh = query.reshape(-1, HEADS, HEAD).astype(jnp.float32)
        kh = keys.reshape(-1, K, HEADS, HEAD).astype(jnp.float32)
        vh = values.reshape(-1, K, HEADS, HEAD).astype(jnp.float32)
        score = jnp.einsum('nhd,nkhd->nhk', qh, kh) / jnp.sqrt(jnp.float32(HEAD))
        expo = jnp.exp(score)
        weights = (expo / lax.optimization_barrier(jnp.sum(expo, axis=-1, keepdims=True))).astype(jnp.bfloat16)
        att = jnp.einsum('nhk,nkhd->nhd', weights.astype(jnp.float32), vh).astype(jnp.bfloat16).reshape(-1, W)
        emb = (jnp.dot(att, w_out, preferred_element_type=jnp.float32) + jnp.dot(self_mem, w_self, preferred_element_type=jnp.float32)).astype(jnp.bfloat16)
        te_msg = encode(times[:, None] - nbr_times[:, :, 0], freq, phase).astype(jnp.bfloat16).reshape(-1, TD)
        edge_two = jnp.broadcast_to(edges[:, None], (edges.shape[0], 2, EF)).reshape(-1, EF)
        msg = jnp.dot(self_mem, w_msg_self, preferred_element_type=jnp.float32) + jnp.dot(other, w_msg_other, preferred_element_type=jnp.float32) + jnp.dot(te_msg, w_msg_time, preferred_element_type=jnp.float32) + jnp.dot(edge_two, w_msg_edge, preferred_element_type=jnp.float32)
        return (emb.reshape(-1, 2, W), msg, self_rows.reshape(-1))
    embedding, msg, dest = lax.map(block, (self_slot.reshape(PEERS, EV_DEV, 2), nbr_slot.reshape(PEERS, EV_DEV, 2, K), ev_time.reshape(PEERS, EV_DEV), nbr_time.reshape(PEERS, EV_DEV, 2, K), edge_feat.reshape(PEERS, EV_DEV, EF), nbr_table, self_table))
    embedding = embedding.reshape(EVENTS, 2, W)
    total = jnp.zeros((NODES, MSG), jnp.float32).at[dest.reshape(-1)].add(msg.reshape(-1, MSG))
    count = jnp.zeros((NODES,), jnp.float32).at[dest.reshape(-1)].add(jnp.ones((dest.size,), jnp.float32))

    def update(args):
        tot, cnt, state = args
        mean = (tot / jnp.maximum(cnt, 1.0)[:, None]).astype(jnp.bfloat16)
        gi = jnp.dot(mean, w_in.reshape(MSG, 3 * W), preferred_element_type=jnp.float32).reshape(-1, 3, W)
        gh = jnp.dot(state, w_hid.reshape(W, 3 * W), preferred_element_type=jnp.float32).reshape(-1, 3, W)
        reset = jax.nn.sigmoid(gi[:, 0] + gh[:, 0])
        gate = jax.nn.sigmoid(gi[:, 1] + gh[:, 1])
        cand = jnp.tanh(gi[:, 2] + reset * gh[:, 2])
        old = state.astype(jnp.float32)
        fresh = (1.0 - gate) * cand + gate * old
        return jnp.where(cnt[:, None] > 0, fresh, old).astype(jnp.bfloat16)
    memory_out = lax.map(update, (total.reshape(PEERS, ROWS_DEV, MSG), count.reshape(PEERS, ROWS_DEV), memory.reshape(PEERS, ROWS_DEV, W))).reshape(NODES, W)
    return (embedding, memory_out)
```

```python
import functools

import jax
import jax.numpy as jnp
from jax import lax
from jax.experimental import pallas as pl
from jax.experimental.pallas import tpu as pltpu
from jax.sharding import PartitionSpec as P

MESH = pl.DeviceIdType.MESH
F32 = jnp.float32
BF16 = jnp.bfloat16
HEADS = 8
X, Y, Z = 4, 4, 8
PLANE = X * Y
W = 512
ROWS = 2048
HALF = W // 2
MSGW = W + 128
DZ_ORDER = (4, 3, 5, 2, 6, 1, 7)
AHEAD = 4
LAG_C, LAG_D = 2, 3
TICKS = PLANE + LAG_D
TICK_SELF, TICK_BACK, TICK_GRU = 2, 6, 11
GRU_TICKS, GRU_TILES = 4, 2


def dot(a, b):
    return jnp.dot(a, b, preferred_element_type=F32)


def iota(shape, dim):
    return lax.broadcasted_iota(jnp.int32, shape, dim)


def onehot(mask):
    return jnp.where(mask, 1.0, 0.0).astype(BF16)


def cosine(angle):
    turns = jnp.floor(angle * 0.15915494309189535 + 0.5)
    r = angle - turns * 6.28125
    r = r - turns * 0.0019353071795864769
    h = 0.5 * r
    s = h * h
    poly = 1.6059043836821613e-10
    for coef in (
        -2.5052108385441720e-08,
        2.7557319223985893e-06,
        -1.9841269841269841e-04,
        8.3333333333333333e-03,
        -1.6666666666666666e-01,
        1.0,
    ):
        poly = poly * s + coef
    sine = poly * h
    return 1.0 - 2.0 * sine * sine


def kernel(
    ev, nbt, nslot, sslot, sself, srows, freq, phase, memory, edge, wq_h, wk_h, wv_h, wo_h, ws_h, wms_h, wmo_h, wmt_h, wme_h, win_h, whid_h,
    emb_out, mem_out,
    mem, wq, wk, wv, wo, ws, wms, wmo, wmt, wme, edges, win, whid,
    picks, nbrs, dts, serve, pk, r1, tab, acc, tcol, te, sp, sr1, sp2, st, mb, mr1, mp2, mu, selfs, qm, ebase, att, emb, fresh, lines,
    in_sem, wl, wsd, wrc, s1s, s1r, s2s, s2r, sbs, sbr, selfsem, backsem, tailsem,
):
    me = lax.axis_index("nodes")
    c = lax.axis_index("mp")
    x, y, z = me // (Y * Z), (me // Z) % Y, me % Z
    p = me // Z
    sib = (me, 1 - c)

    def plane(k, sign):
        dx, dy = k // Y, k % Y
        return ((x + X + sign * dx) % X) * Y + (y + Y + sign * dy) % Y

    def to(g):
        return plane((g + 1) % PLANE, 1 - 2 * c)

    def frm(g, core):
        return plane((g + 1) % PLANE, 2 * core - 1)

    def zpeer(dz):
        return (z + dz) % Z

    def zdev(dz):
        return (p * Z + zpeer(dz), c)

    def remote(src, dst, s, r, dev):
        return pltpu.make_async_remote_copy(src, dst, s, r, device_id=dev, device_id_type=MESH)

    def wait(ref, sem):
        pltpu.make_async_copy(ref, ref, sem).wait()

    mem_cp = pltpu.make_async_copy(memory, mem, in_sem.at[0])
    mem_cp.start()
    cols = pl.ds(pl.multiple_of(c * HALF, HALF), HALF)
    rows256 = pl.ds(pl.multiple_of(c * HALF, HALF), HALF)
    rows64 = pl.ds(pl.multiple_of(c * 64, 64), 64)
    shared = [
        (wms_h, wms.at[rows256]), (wmo_h, wmo.at[rows256]), (wmt_h, wmt.at[rows64]), (wme_h, wme.at[rows64]),
        (edge, edges.at[c]), (wq_h, wq.at[:, cols]), (ws_h, ws.at[rows256]), (wk_h, wk.at[:, cols]),
        (wv_h, wv.at[:, cols]), (wo_h, wo.at[rows256]),
    ]
    win_cp = pltpu.make_async_copy(win_h, win, in_sem.at[1])
    whid_cp = pltpu.make_async_copy(whid_h, whid, in_sem.at[2])

    bar = pltpu.get_barrier_semaphore()
    pl.semaphore_signal(bar, inc=1, device_id=sib, device_id_type=MESH)
    for dz in DZ_ORDER:
        pl.semaphore_signal(bar, inc=1, device_id=zdev(dz), device_id_type=MESH)

    def greet(k, _):
        pl.semaphore_signal(bar, inc=1, device_id=(plane(k, 1) * Z + z, c), device_id_type=MESH)
        return 0

    lax.fori_loop(1, PLANE, greet, 0)
    for n, (src, dst) in enumerate(shared):
        pltpu.make_async_copy(src, dst, wl.at[n]).start()
    win_cp.start()
    whid_cp.start()

    def turn(rows):
        full = jnp.concatenate([rows, jnp.zeros((128 - rows.shape[0], 128), jnp.int32)], axis=0)
        return jnp.transpose(full.astype(F32))

    def spread(block, first):
        n = block.shape[0] * 16
        many = jnp.broadcast_to(block[:, None, :], (block.shape[0], 16, 128)).reshape(n, 128)
        take = iota((n, 128), 1) == first + iota((n, 128), 0) % 16
        return jnp.sum(jnp.where(take, many, 0.0), axis=1, keepdims=True)

    def column(line):
        return jnp.transpose(jnp.broadcast_to(line.astype(F32), (128, 128)))

    lanes2048 = iota((128, ROWS), 1).astype(F32)

    def pick(col):
        return dot(onehot(col == lanes2048), mem[...]).astype(BF16)

    picks[...] = turn(srows[...])
    by_node = turn(sself[...])
    high = jnp.floor(by_node * 0.0625)
    parts = jnp.concatenate([high, by_node - 16.0 * high], axis=1).astype(BF16)
    si, sj = iota((256, 128), 0), iota((256, 128), 1)
    node = ((si // 2) % PLANE) * Z + si // 32
    both = dot(onehot(sj == node), parts)
    both = 16.0 * both[:, 0:128] + both[:, 128:256]
    for core in range(2):
        col = jnp.sum(jnp.where(sj == 2 * core + si % 2, both, 0.0), axis=1, keepdims=True)
        wide = jnp.broadcast_to(col, (256, 128))
        serve[core] = wide
        for n in range(2):
            lines[pl.ds(2 * core + n, 1), :] = jnp.transpose(wide[128 * n : 128 * n + 128])[0:1]
    mem_cp.wait()

    def pick_self(n, _):
        r = pl.ds(pl.multiple_of(n * 128, 128), 128)
        sp[r, :] = pick(jnp.tile(serve[c, r, :], (1, ROWS // 128)))
        return 0

    lax.fori_loop(0, 2, pick_self, 0)
    own32 = pl.ds(pl.multiple_of(z * 32, 32), 32)
    own16 = pl.ds(pl.multiple_of(z * 16, 16), 16)
    plane16 = pl.ds(pl.multiple_of(p * 16, 16), 16)
    sr1[own32, :] = sp[own32, :]
    pl.semaphore_wait(bar, Z - 1 + PLANE - 1 + 1)
    for dz in DZ_ORDER:
        blk = pl.ds(pl.multiple_of(zpeer(dz) * 32, 32), 32)
        remote(sp.at[blk], sr1.at[own32], selfsem.at[0], selfsem.at[1], zdev(dz)).start()
    for n, (src, dst) in enumerate(shared):
        remote(src, dst, wsd.at[n], wrc.at[n], sib).start()

    def step_a(g):
        pk[g] = pick(spread(picks[pl.ds(pl.multiple_of(to(g) * Z, Z), Z), :], 16 * c))
        r1[g, own16, :] = pk[g, own16, :]
        for dz in DZ_ORDER:
            blk = pl.ds(pl.multiple_of(zpeer(dz) * 16, 16), 16)
            remote(pk.at[g, blk], r1.at[g, own16], s1s.at[g], s1r.at[g], zdev(dz)).start()

    def step_b(g):
        wait(r1.at[g, pl.ds(0, 112)], s1r.at[g])

        @pl.when(g < PLANE - 1)
        def _():
            remote(r1.at[g], tab.at[c, p], s2s.at[g], s2r.at[g], (to(g) * Z + z, c)).start()

        @pl.when(g == PLANE - 1)
        def _():
            remote(r1.at[g], tab.at[c, p], sbs.at[g], sbr.at[g], sib).start()
            pltpu.make_async_copy(r1.at[g], tab.at[c, p], s2r.at[g]).start()

    def step_c(g):
        part = tab.at[c, frm(g, c)]
        wait(part, s2r.at[g])

        @pl.when(g < PLANE - 1)
        def _():
            remote(part, part, sbs.at[g], sbr.at[g], sib).start()

    lanes128 = iota((256, 128), 1).astype(F32)

    def step_d(g):
        src0, src1 = frm(g, 0), frm(g, 1)
        wait(tab.at[1 - c, frm(g, 1 - c)], sbr.at[g])
        table = jnp.concatenate([tab[0, src0], tab[1, src1]], axis=0)
        base0, base1 = (src0 * 128).astype(F32), (src1 * 128 + ROWS).astype(F32)

        def tile(m, _):
            r = pl.ds(pl.multiple_of(m * 256, 256), 256)
            at = tcol[r, :]
            oh = jnp.concatenate([onehot(at - base0 == lanes128), onehot(at - base1 == lanes128)], axis=1)
            acc[r, :] = acc[r, :] + dot(oh, table).astype(BF16)
            return 0

        lax.fori_loop(0, 8, tile, 0)

    def first(g, _):
        step_a(g)
        return 0

    lax.fori_loop(0, AHEAD, first, 0)

    slot = nslot[c]
    nbrs[...] = turn((slot % 32 // 16) * ROWS + (slot // 32) * 16 + slot % 16)
    dts[...] = turn(ev[...] - nbt[c])

    def prepare(b, _):
        r = pl.ds(pl.multiple_of(b * 256, 256), 256)
        e = pl.ds(pl.multiple_of(b * 16, 16), 16)
        tcol[r, :] = jnp.broadcast_to(spread(nbrs[e, :], 0), (256, 128))
        te[r, :] = cosine(spread(dts[e, :], 0) * freq[...] + phase[...]).astype(BF16)
        acc[r, :] = jnp.zeros((256, W), BF16)
        return 0

    lax.fori_loop(0, 8, prepare, 0)

    wait(sr1.at[pl.ds(0, 224)], selfsem.at[1])
    out_i, in_j = iota((256, 256), 0), iota((256, 256), 1)
    to_plane = onehot(in_j == ((out_i // 2) % Z) * 32 + (out_i // 16) * 2 + out_i % 2)
    sp2[...] = dot(to_plane, sr1[...]).astype(BF16)
    st[c, plane16, :] = sp2[plane16, :]

    def self_plane(k, _):
        q = plane(k, 1)
        blk = pl.ds(pl.multiple_of(q * 16, 16), 16)
        remote(sp2.at[blk], st.at[c, plane16], selfsem.at[2], selfsem.at[3], (q * Z + z, c)).start()
        return 0

    lax.fori_loop(1, PLANE, self_plane, 0)

    def do_self():
        wait(st.at[c, pl.ds(0, 240)], selfsem.at[3])
        remote(st.at[c], st.at[c], selfsem.at[4], selfsem.at[5], sib).start()
        for n, (src, dst) in enumerate(shared):
            pltpu.make_async_copy(src, dst, wl.at[n]).wait()
            remote(src, dst, wsd.at[n], wrc.at[n], sib).wait()
        wait(st.at[1 - c], selfsem.at[5])
        table = jnp.concatenate([st[0], st[1]], axis=0)
        lanes512 = iota((128, W), 1).astype(F32)

        ends = (sslot[...] % 4 // 2) * 256 + (sslot[...] // 4) * 2 + sslot[...] % 2
        for n in range(2):
            at = jnp.tile(column(ends[n : n + 1]), (1, 4))
            selfs[pl.ds(128 * n, 128), :] = dot(onehot(at == lanes512), table).astype(BF16)
        mine = selfs[...]
        other = jnp.concatenate([mine[128:256], mine[0:128]], axis=0)
        te_m = jnp.concatenate(
            [cosine(column(ev[...] - nbt[n, 0:1]) * freq[...] + phase[...]).astype(BF16) for n in range(2)], axis=0
        )
        msg = dot(mine, wms[...]) + dot(other, wmo[...]) + dot(te_m, wmt[...])
        feats = jnp.concatenate([edges[0], edges[1]], axis=0)
        shared_part = lax.dot_general(feats, wme[...], (((0,), (0,)), ((), ())), preferred_element_type=F32)
        msg = msg + jnp.concatenate([shared_part, shared_part], axis=0)
        slots = jnp.concatenate([ends[0:1], ends[1:2]], axis=1)
        member = onehot(jnp.broadcast_to(slots, (256, 256)) == out_i + c * 256)
        high = msg.astype(BF16)
        low = (msg - high.astype(F32)).astype(BF16)
        mb[:, pl.ds(0, W)] = (dot(member, high) + dot(member, low)).astype(BF16)
        mb[:, pl.ds(W, 128)] = dot(member, jnp.ones((256, 128), BF16)).astype(BF16)
        mr1[plane16, :] = mb[plane16, :]

        def back_plane(k, _):
            q = plane(k, 1)
            blk = pl.ds(pl.multiple_of(q * 16, 16), 16)
            remote(mb.at[blk], mr1.at[plane16], backsem.at[0], backsem.at[1], (q * Z + z, c)).start()
            return 0

        lax.fori_loop(1, PLANE, back_plane, 0)
        ours = selfs[pl.ds(pl.multiple_of(c * 128, 128), 128), :]
        te_s = jnp.broadcast_to(cosine(phase[...]).astype(BF16), (8, 128))
        query = (dot(ours, wq[pl.ds(0, W), :]) + dot(te_s, wq[pl.ds(W, 128), :])[0:1]).astype(BF16)
        ebase[...] = dot(ours, ws[...])
        head = iota((16, W), 1) // (W // HEADS)
        for t in range(8):
            part = query[16 * t : 16 * t + 16]
            for h in range(HEADS):
                qm[t, pl.ds(16 * h, 16), :] = jnp.where(head == h, part, jnp.zeros_like(part))

    def do_back():
        wait(mr1.at[pl.ds(0, 240)], backsem.at[1])
        to_z = onehot(in_j == ((out_i // 2) % PLANE) * 16 + (out_i // 32) * 2 + out_i % 2)
        mp2[...] = dot(to_z, mr1[...]).astype(BF16)
        mu[c, own32, :] = mp2[own32, :]
        for dz in DZ_ORDER:
            blk = pl.ds(pl.multiple_of(zpeer(dz) * 32, 32), 32)
            remote(mp2.at[blk], mu.at[c, own32], backsem.at[2], backsem.at[3], zdev(dz)).start()

    def do_share():
        wait(mu.at[c, pl.ds(0, 224)], backsem.at[3])
        remote(mu.at[c], mu.at[c], backsem.at[4], backsem.at[5], sib).start()
        win_cp.wait()
        whid_cp.wait()
        wait(mu.at[1 - c], backsem.at[5])

    def gru(m):
        r = pl.ds(pl.multiple_of(m * 256, 256), 256)
        local = (iota((256, 128), 0) + m * 256).astype(F32)
        hit = jnp.concatenate(
            [onehot(jnp.broadcast_to(lines[pl.ds(n, 1), :], (256, 128)) == local) for n in range(4)], axis=1
        )
        sums = dot(hit, jnp.concatenate([mu[0], mu[1]], axis=0))
        count = sums[:, W : W + 128]
        inv = jnp.maximum(count, 1.0)
        mean = jnp.concatenate([sums[:, 128 * n : 128 * n + 128] / inv for n in range(4)], axis=1).astype(BF16)
        state = mem[r, :]
        gi = [dot(mean, win[g]) for g in range(3)]
        gh = [dot(state, whid[g]) for g in range(3)]
        reset = jax.nn.sigmoid(gi[0] + gh[0])
        gate = jax.nn.sigmoid(gi[1] + gh[1])
        cand = jnp.tanh(gi[2] + reset * gh[2])
        old = mem[r, cols].astype(F32)
        new = (1.0 - gate) * cand + gate * old
        some = jnp.concatenate([count, count], axis=1) > 0
        fresh[r, :] = jnp.where(some, new, old).astype(BF16)

    def tick(i, _):
        @pl.when(i < PLANE)
        def _():
            step_b(i)

        @pl.when(i + AHEAD < PLANE)
        def _():
            step_a(i + AHEAD)

        @pl.when(i == TICK_SELF)
        def _():
            do_self()

        @pl.when(i == TICK_BACK)
        def _():
            do_back()

        @pl.when((i >= LAG_C) & (i < PLANE + LAG_C))
        def _():
            step_c(i - LAG_C)

        @pl.when(i >= LAG_D)
        def _():
            step_d(i - LAG_D)

        @pl.when(i == TICK_GRU)
        def _():
            do_share()

        @pl.when((i >= TICK_GRU) & (i < TICK_GRU + GRU_TICKS))
        def _():
            def tile(n, _):
                gru((i - TICK_GRU) * GRU_TILES + n)
                return 0

            lax.fori_loop(0, GRU_TILES, tile, 0)

        return 0

    lax.fori_loop(0, TICKS, tick, 0)
    fresh_cp = pltpu.make_async_copy(fresh, mem_out, tailsem.at[2])
    fresh_cp.start()

    same = (iota((128, 256), 0) % 16) == (iota((128, 256), 1) // 16)
    headcol = iota((16, W), 1) // (W // HEADS)

    def attend(t, _):
        r = pl.ds(pl.multiple_of(t * 256, 256), 256)
        nb, tn = acc[r, :], te[r, :]
        keys = (dot(nb, wk[pl.ds(0, W), :]) + dot(tn, wk[pl.ds(W, 128), :])).astype(BF16)
        vals = (dot(nb, wv[pl.ds(0, W), :]) + dot(tn, wv[pl.ds(W, 128), :])).astype(BF16)
        score = lax.dot_general(qm[t], keys, (((1,), (1,)), ((), ())), preferred_element_type=F32) * 0.125
        expo = jnp.where(same, jnp.exp(score), 0.0)
        weights = (expo / jnp.sum(expo, axis=1, keepdims=True)).astype(BF16)
        full = dot(weights, vals)
        out = jnp.zeros((16, W), F32)
        for h in range(HEADS):
            out = jnp.where(headcol == h, full[16 * h : 16 * h + 16], out)
        att[pl.ds(pl.multiple_of(t * 16, 16), 16), :] = out.astype(BF16)
        return 0

    lax.fori_loop(0, 8, attend, 0)
    mine128 = pl.ds(pl.multiple_of(c * 128, 128), 128)
    emb[mine128, :] = (dot(att[...], wo[...]) + ebase[...]).astype(BF16)
    send = remote(emb.at[mine128], emb.at[mine128], tailsem.at[0], tailsem.at[1], sib)
    send.start()

    def drain(g, _):
        wait(pk.at[g, pl.ds(0, 112)], s1s.at[g])

        @pl.when(g < PLANE - 1)
        def _():
            wait(r1.at[g], s2s.at[g])

        wait(r1.at[g], sbs.at[g])
        return 0

    lax.fori_loop(0, PLANE, drain, 0)
    wait(sp.at[pl.ds(0, 224)], selfsem.at[0])
    wait(sp2.at[pl.ds(0, 240)], selfsem.at[2])
    wait(st.at[c], selfsem.at[4])
    wait(mb.at[pl.ds(0, 240)], backsem.at[0])
    wait(mp2.at[pl.ds(0, 224)], backsem.at[2])
    wait(mu.at[c], backsem.at[4])
    send.wait()
    emb_cp = pltpu.make_async_copy(emb, emb_out, tailsem.at[3])
    emb_cp.start()
    fresh_cp.wait()
    emb_cp.wait()


def deliver(emb, fresh, emb_out, mem_out, buf, load, store):
    parts = [pl.ds(ROWS // 4 * n, ROWS // 4) for n in range(4)]
    loads = [pltpu.make_async_copy(fresh.at[r], buf.at[r], load.at[n]) for n, r in enumerate(parts)]
    stores = [pltpu.make_async_copy(buf.at[r], mem_out.at[r], store.at[n]) for n, r in enumerate(parts)]
    for cp in loads:
        cp.start()
    for n in range(2):
        emb_out[:, n, :] = emb[pl.ds(128 * n, 128), :]
    for n in range(4):
        loads[n].wait()
        stores[n].start()
    for cp in stores:
        cp.wait()


def per_device(
    memory, ev_time, nbr_time, edge_feat, self_slot, nbr_slot, serve_self, serve_rows, freq, phase,
    w_query, w_key, w_value, w_out, w_self, w_msg_self, w_msg_other, w_msg_time, w_msg_edge, w_in, w_hid,
):
    vmem = pl.BlockSpec(memory_space=pltpu.VMEM)
    hbm = pl.BlockSpec(memory_space=pl.ANY)
    v = lambda *s: pltpu.VMEM(s, BF16)
    vf = lambda *s: pltpu.VMEM(s, F32)
    dma = lambda n: pltpu.SemaphoreType.DMA((n,))
    emb, fresh = pl.pallas_call(
        kernel,
        out_shape=(jax.ShapeDtypeStruct((256, W), BF16), jax.ShapeDtypeStruct((ROWS, HALF), BF16)),
        in_specs=[vmem] * 8 + [hbm] * 13,
        out_specs=(hbm, hbm),
        scratch_shapes=[
            v(ROWS, W), v(640, W), v(640, W), v(640, W), v(W, W), v(W, W), v(W, W), v(W, W), v(128, W), v(128, W),
            v(2, 64, 128), v(3, W, HALF), v(3, W, HALF),
            vf(128, 128), vf(128, 128), vf(128, 128), vf(2, 256, 128),
            v(16, 128, W), v(16, 128, W), v(2, 16, 128, W), v(2048, W), vf(2048, 128), v(2048, 128),
            v(256, W), v(256, W), v(256, W), v(2, 256, W), v(256, MSGW), v(256, MSGW), v(256, MSGW), v(2, 256, MSGW),
            v(256, W), v(8, 128, W), vf(128, W), v(128, W), v(256, W), v(ROWS, HALF), vf(4, 128),
            dma(3), dma(10), dma(10), dma(10), dma(16), dma(16), dma(16), dma(16), dma(16), dma(16),
            dma(6), dma(6), dma(4),
        ],
        compiler_params=pltpu.CompilerParams(
            collective_id=0, has_side_effects=True, vmem_limit_bytes=60 * 1024 * 1024
        ),
    )(
        ev_time.reshape(1, 128), nbr_time.transpose(1, 2, 0), nbr_slot.transpose(1, 2, 0), self_slot.T,
        serve_self[0].T, serve_rows[0].T, freq.reshape(1, 128), phase.reshape(1, 128), memory, edge_feat.T,
        w_query, w_key, w_value, w_out, w_self,
        w_msg_self, w_msg_other, w_msg_time, w_msg_edge, w_in.transpose(1, 0, 2), w_hid.transpose(1, 0, 2),
    )
    return pl.pallas_call(
        deliver,
        out_shape=(jax.ShapeDtypeStruct((128, 2, W), BF16), jax.ShapeDtypeStruct((ROWS, HALF), BF16)),
        in_specs=[vmem, hbm],
        out_specs=(vmem, hbm),
        scratch_shapes=[v(ROWS, HALF), dma(4), dma(4)],
    )(emb, fresh)


def solution(mesh):
    return jax.shard_map(
        per_device,
        mesh=mesh,
        in_specs=(
            P("nodes", None), P("nodes"), P("nodes", None, None), P("nodes", "mp"), P("nodes", None),
            P("nodes", None, None), P("nodes", None, None), P("nodes", None, None), P(), P(),
            P(None, "mp"), P(None, "mp"), P(None, "mp"), P("mp", None), P("mp", None), P("mp", None),
            P("mp", None), P("mp", None), P("mp", None), P(None, None, "mp"), P(None, None, "mp"),
        ),
        out_specs=(P("nodes", None, None), P("nodes", "mp")),
        check_vma=False,
    )
```

```python
import functools

import jax
import jax.numpy as jnp
from jax import lax
from jax.experimental import pallas as pl
from jax.experimental.pallas import tpu as pltpu
from jax.sharding import PartitionSpec as P

MESH = pl.DeviceIdType.MESH
F32 = jnp.float32
BF16 = jnp.bfloat16
HEADS = 8
X, Y, Z = 4, 4, 8
PLANE = X * Y
W = 512
ROWS = 2048
HALF = W // 2
MSGW = W + 128
DZ_ORDER = (4, 3, 5, 2, 6, 1, 7)
AHEAD = 4
LAG_C, LAG_D = 2, 3
TICKS = PLANE + LAG_D
TICK_SELF, TICK_BACK, TICK_GRU = 2, 6, 11
GRU_TICKS, GRU_TILES = 2, 4


def dot(a, b):
    return jnp.dot(a, b, preferred_element_type=F32)


def iota(shape, dim):
    return lax.broadcasted_iota(jnp.int32, shape, dim)


def onehot(mask):
    return jnp.where(mask, 1.0, 0.0).astype(BF16)


def cosine(angle):
    turns = jnp.floor(angle * 0.15915494309189535 + 0.5)
    r = angle - turns * 6.28125
    r = r - turns * 0.0019353071795864769
    h = 0.5 * r
    s = h * h
    poly = 1.6059043836821613e-10
    for coef in (
        -2.5052108385441720e-08,
        2.7557319223985893e-06,
        -1.9841269841269841e-04,
        8.3333333333333333e-03,
        -1.6666666666666666e-01,
        1.0,
    ):
        poly = poly * s + coef
    sine = poly * h
    return 1.0 - 2.0 * sine * sine


def kernel(
    ev, nbt, nslot, sslot, sself, srows, freq, phase, memory, edge, wq_h, wk_h, wv_h, wo_h, ws_h, wms_h, wmo_h, wmt_h, wme_h, win_h, whid_h,
    emb_out, mem_out,
    mem, wq, wk, wv, wo, ws, wms, wmo, wmt, wme, edges, win, whid,
    picks, nbrs, dts, serve, pk, r1, tab, acc, tcol, te, sp, sr1, sp2, st, mb, mr1, mp2, mu, selfs, qm, ebase, att, emb, fresh, lines, keyline, ghs, slotrows,
    in_sem, wl, wsd, wrc, s1s, s1r, s2s, s2r, sbs, sbr, selfsem, backsem, tailsem,
):
    me = lax.axis_index("nodes")
    c = lax.axis_index("mp")
    x, y, z = me // (Y * Z), (me // Z) % Y, me % Z
    p = me // Z
    sib = (me, 1 - c)

    def plane(k, sign):
        dx, dy = k // Y, k % Y
        return ((x + X + sign * dx) % X) * Y + (y + Y + sign * dy) % Y

    def to(g):
        return plane((g + 1) % PLANE, 1 - 2 * c)

    def frm(g, core):
        return plane((g + 1) % PLANE, 2 * core - 1)

    def zpeer(dz):
        return (z + dz) % Z

    def zdev(dz):
        return (p * Z + zpeer(dz), c)

    def remote(src, dst, s, r, dev):
        return pltpu.make_async_remote_copy(src, dst, s, r, device_id=dev, device_id_type=MESH)

    def wait(ref, sem):
        pltpu.make_async_copy(ref, ref, sem).wait()

    mem_cp = pltpu.make_async_copy(memory, mem, in_sem.at[0])
    mem_cp.start()
    cols = pl.ds(pl.multiple_of(c * HALF, HALF), HALF)
    rows256 = pl.ds(pl.multiple_of(c * HALF, HALF), HALF)
    rows64 = pl.ds(pl.multiple_of(c * 64, 64), 64)
    shared = [
        (wms_h, wms.at[rows256]), (wmo_h, wmo.at[rows256]), (wmt_h, wmt.at[rows64]), (wme_h, wme.at[rows64]),
        (edge, edges.at[c]), (wq_h, wq.at[:, cols]), (ws_h, ws.at[rows256]), (wk_h, wk.at[:, cols]),
        (wv_h, wv.at[:, cols]), (wo_h, wo.at[rows256]),
    ]
    win_cp = pltpu.make_async_copy(win_h, win, in_sem.at[1])
    whid_cp = pltpu.make_async_copy(whid_h, whid, in_sem.at[2])

    bar = pltpu.get_barrier_semaphore()
    pl.semaphore_signal(bar, inc=1, device_id=sib, device_id_type=MESH)
    for dz in DZ_ORDER:
        pl.semaphore_signal(bar, inc=1, device_id=zdev(dz), device_id_type=MESH)

    def greet(k, _):
        pl.semaphore_signal(bar, inc=1, device_id=(plane(k, 1) * Z + z, c), device_id_type=MESH)
        return 0

    lax.fori_loop(1, PLANE, greet, 0)
    for n, (src, dst) in enumerate(shared):
        pltpu.make_async_copy(src, dst, wl.at[n]).start()
    win_cp.start()
    whid_cp.start()

    def turn(rows):
        full = jnp.concatenate([rows, jnp.zeros((128 - rows.shape[0], 128), jnp.int32)], axis=0)
        return jnp.transpose(full.astype(F32))

    def spread(block, first):
        n = block.shape[0] * 16
        many = jnp.broadcast_to(block[:, None, :], (block.shape[0], 16, 128)).reshape(n, 128)
        take = iota((n, 128), 1) == first + iota((n, 128), 0) % 16
        return jnp.sum(jnp.where(take, many, 0.0), axis=1, keepdims=True)

    def column(line):
        return jnp.transpose(jnp.broadcast_to(line.astype(F32), (128, 128)))

    lanes2048 = iota((1, ROWS), 1).astype(F32)

    def pick(col):
        return dot(onehot(col == lanes2048), mem[...]).astype(BF16)

    picks[...] = turn(srows[...])
    by_node = turn(sself[...])
    high = jnp.floor(by_node * 0.0625)
    parts = jnp.concatenate([high, by_node - 16.0 * high], axis=1).astype(BF16)
    si, sj = iota((256, 128), 0), iota((256, 128), 1)
    node = ((si // 2) % PLANE) * Z + si // 32
    both = dot(onehot(sj == node), parts)
    both = 16.0 * both[:, 0:128] + both[:, 128:256]
    for core in range(2):
        col = jnp.sum(jnp.where(sj == 2 * core + si % 2, both, 0.0), axis=1, keepdims=True)
        wide = jnp.broadcast_to(col, (256, 128))
        serve[core] = wide
        for n in range(2):
            lines[pl.ds(2 * core + n, 1), :] = jnp.transpose(wide[128 * n : 128 * n + 128])[0:1]
    mem_cp.wait()

    def pick_self(core, _):
        sp[core] = pick(serve[core, :, pl.ds(0, 1)])
        return 0

    pick_self(c, 0)
    own32 = pl.ds(pl.multiple_of(z * 32, 32), 32)
    own16 = pl.ds(pl.multiple_of(z * 16, 16), 16)
    plane16 = pl.ds(pl.multiple_of(p * 16, 16), 16)
    sr1[own32, :] = sp[c, own32, :]
    pl.semaphore_wait(bar, Z - 1 + PLANE - 1 + 1)
    for dz in DZ_ORDER:
        blk = pl.ds(pl.multiple_of(zpeer(dz) * 32, 32), 32)
        remote(sp.at[c, blk], sr1.at[own32], selfsem.at[0], selfsem.at[1], zdev(dz)).start()
    for n, (src, dst) in enumerate(shared):
        remote(src, dst, wsd.at[n], wrc.at[n], sib).start()

    def step_a(j):
        rows = [picks[pl.ds(pl.multiple_of(to(2 * j + n) * Z, Z), Z), :] for n in range(2)]
        got = pick(spread(jnp.concatenate(rows, axis=0), 16 * c))
        for n in range(2):
            g = 2 * j + n
            pk[g] = got[128 * n : 128 * n + 128]
        for n in range(2):
            g = 2 * j + n
            r1[g, own16, :] = pk[g, own16, :]
            for dz in DZ_ORDER:
                blk = pl.ds(pl.multiple_of(zpeer(dz) * 16, 16), 16)
                remote(pk.at[g, blk], r1.at[g, own16], s1s.at[g], s1r.at[g], zdev(dz)).start()

    def step_b(g):
        wait(r1.at[g, pl.ds(0, 112)], s1r.at[g])

        @pl.when(g < PLANE - 1)
        def _():
            remote(r1.at[g], tab.at[c, p], s2s.at[g], s2r.at[g], (to(g) * Z + z, c)).start()

        @pl.when(g == PLANE - 1)
        def _():
            remote(r1.at[g], tab.at[c, p], sbs.at[g], sbr.at[g], sib).start()
            pltpu.make_async_copy(r1.at[g], tab.at[c, p], s2r.at[g]).start()

    def step_c(g):
        part = tab.at[c, frm(g, c)]
        wait(part, s2r.at[g])

        @pl.when(g < PLANE - 1)
        def _():
            remote(part, part, sbs.at[g], sbr.at[g], sib).start()

    lanes128 = iota((1, 128), 1).astype(F32)

    def step_d(j):
        tables, marks = [], []
        for n in range(2):
            g = 2 * j + n
            wait(tab.at[1 - c, frm(g, 1 - c)], sbr.at[g])
        for n in range(2):
            for core in range(2):
                src = frm(2 * j + n, core)
                tables.append(tab[core, src])
                marks.append(lanes128 + (src * 128 + core * ROWS).astype(F32))
        table = jnp.concatenate(tables, axis=0)

        def tile(m, _):
            r = pl.ds(pl.multiple_of(m * 512, 512), 512)
            at = tcol[r, :]
            oh = jnp.concatenate([onehot(at == mark) for mark in marks], axis=1)
            acc[r, :] = acc[r, :] + dot(oh, table).astype(BF16)
            return 0

        lax.fori_loop(0, 4, tile, 0)

    def first(g, _):
        step_a(g)
        return 0

    lax.fori_loop(0, AHEAD // 2, first, 0)
    pick_self(1 - c, 0)

    slot = nslot[c]
    nbrs[...] = turn((slot % 32 // 16) * ROWS + (slot // 32) * 16 + slot % 16)
    dts[...] = turn(ev[...] - nbt[c])

    def prepare(b, _):
        r = pl.ds(pl.multiple_of(b * 256, 256), 256)
        e = pl.ds(pl.multiple_of(b * 16, 16), 16)
        tcol[r, :] = jnp.broadcast_to(spread(nbrs[e, :], 0), (256, 128))
        te[r, :] = cosine(spread(dts[e, :], 0) * freq[...] + phase[...]).astype(BF16)
        acc[r, :] = jnp.zeros((256, W), BF16)
        return 0

    lax.fori_loop(0, 8, prepare, 0)

    wait(sr1.at[pl.ds(0, 224)], selfsem.at[1])
    out_i, in_j = iota((256, 256), 0), iota((256, 256), 1)
    to_plane = onehot(in_j == ((out_i // 2) % Z) * 32 + (out_i // 16) * 2 + out_i % 2)
    sp2[...] = dot(to_plane, sr1[...]).astype(BF16)
    st[c, plane16, :] = sp2[plane16, :]

    def self_plane(k, _):
        q = plane(k, 1)
        blk = pl.ds(pl.multiple_of(q * 16, 16), 16)
        remote(sp2.at[blk], st.at[c, plane16], selfsem.at[2], selfsem.at[3], (q * Z + z, c)).start()
        return 0

    lax.fori_loop(1, PLANE, self_plane, 0)
    whid_cp.wait()

    def hidden(n, _):
        for g in range(3):
            ghs[g, pl.ds(pl.multiple_of(n * 256, 256), 256), :] = dot(sp[n], whid[g])
        return 0

    lax.fori_loop(0, 2, hidden, 0)

    def do_self():
        wait(st.at[c, pl.ds(0, 240)], selfsem.at[3])
        remote(st.at[c], st.at[c], selfsem.at[4], selfsem.at[5], sib).start()
        for n, (src, dst) in enumerate(shared):
            pltpu.make_async_copy(src, dst, wl.at[n]).wait()
            remote(src, dst, wsd.at[n], wrc.at[n], sib).wait()
        wait(st.at[1 - c], selfsem.at[5])
        table = jnp.concatenate([st[0], st[1]], axis=0)
        lanes512 = iota((128, W), 1).astype(F32)

        ends = (sslot[...] % 4 // 2) * 256 + (sslot[...] // 4) * 2 + sslot[...] % 2
        for n in range(2):
            at = jnp.tile(column(ends[n : n + 1]), (1, 4))
            selfs[pl.ds(128 * n, 128), :] = dot(onehot(at == lanes512), table).astype(BF16)
        mine = selfs[...]
        other = jnp.concatenate([mine[128:256], mine[0:128]], axis=0)
        te_m = jnp.concatenate(
            [cosine(column(ev[...] - nbt[n, 0:1]) * freq[...] + phase[...]).astype(BF16) for n in range(2)], axis=0
        )
        msg = dot(mine, wms[...]) + dot(other, wmo[...]) + dot(te_m, wmt[...])
        feats = jnp.concatenate([edges[0], edges[1]], axis=0)
        shared_part = lax.dot_general(feats, wme[...], (((0,), (0,)), ((), ())), preferred_element_type=F32)
        msg = msg + jnp.concatenate([shared_part, shared_part], axis=0)
        slots = jnp.concatenate([ends[0:1], ends[1:2]], axis=1)
        member = onehot(jnp.broadcast_to(slots, (256, 256)) == out_i + c * 256)
        high = msg.astype(BF16)
        low = (msg - high.astype(F32)).astype(BF16)
        mb[:, pl.ds(0, W)] = (dot(member, high) + dot(member, low)).astype(BF16)
        mb[:, pl.ds(W, 128)] = dot(member, jnp.ones((256, 128), BF16)).astype(BF16)
        mr1[plane16, :] = mb[plane16, :]

        def back_plane(k, _):
            q = plane(k, 1)
            blk = pl.ds(pl.multiple_of(q * 16, 16), 16)
            remote(mb.at[blk], mr1.at[plane16], backsem.at[0], backsem.at[1], (q * Z + z, c)).start()
            return 0

        lax.fori_loop(1, PLANE, back_plane, 0)
        ours = selfs[pl.ds(pl.multiple_of(c * 128, 128), 128), :]
        te_s = jnp.broadcast_to(cosine(phase[...]).astype(BF16), (8, 128))
        query = (dot(ours, wq[pl.ds(0, W), :]) + dot(te_s, wq[pl.ds(W, 128), :])[0:1]).astype(BF16)
        ebase[...] = dot(ours, ws[...])
        head = iota((16, W), 1) // (W // HEADS)
        for t in range(8):
            part = query[16 * t : 16 * t + 16]
            for h in range(HEADS):
                qm[t, pl.ds(16 * h, 16), :] = jnp.where(head == h, part, jnp.zeros_like(part))

    def do_back():
        wait(mr1.at[pl.ds(0, 240)], backsem.at[1])
        to_z = onehot(in_j == ((out_i // 2) % PLANE) * 16 + (out_i // 32) * 2 + out_i % 2)
        mp2[...] = dot(to_z, mr1[...]).astype(BF16)
        mu[c, own32, :] = mp2[own32, :]
        for dz in DZ_ORDER:
            blk = pl.ds(pl.multiple_of(zpeer(dz) * 32, 32), 32)
            remote(mp2.at[blk], mu.at[c, own32], backsem.at[2], backsem.at[3], zdev(dz)).start()

    def do_share():
        wait(mu.at[c, pl.ds(0, 224)], backsem.at[3])
        remote(mu.at[c], mu.at[c], backsem.at[4], backsem.at[5], sib).start()
        win_cp.wait()
        line = jnp.concatenate([lines[pl.ds(n, 1), :] for n in range(4)], axis=1)
        col = jnp.concatenate([serve[0], serve[1]], axis=0)
        same = jnp.tile(col, (1, 4)) == line
        before = same & (iota((512, 512), 0) < iota((512, 512), 1))
        rank = jnp.sum(jnp.where(before, 1.0, 0.0), axis=0, keepdims=True)
        keyline[...] = jnp.where(rank == 0.0, line, -1.0)
        wait(mu.at[1 - c], backsem.at[5])

        def update(n, _):
            r = pl.ds(pl.multiple_of(n * 256, 256), 256)
            hits = onehot(jnp.tile(serve[n], (1, 4)) == line)
            sums = dot(hits, jnp.concatenate([mu[0], mu[1]], axis=0))
            count = sums[:, W : W + 128]
            most = jnp.maximum(count, 1.0)
            mean = jnp.concatenate([sums[:, 128 * k : 128 * k + 128] / most for k in range(4)], axis=1).astype(BF16)
            gi = [dot(mean, win[g]) for g in range(3)]
            gh = [ghs[g, r, :] for g in range(3)]
            reset = jax.nn.sigmoid(gi[0] + gh[0])
            gate = jax.nn.sigmoid(gi[1] + gh[1])
            cand = jnp.tanh(gi[2] + reset * gh[2])
            old = sp[n, :, cols].astype(F32)
            new = (1.0 - gate) * cand + gate * old
            some = jnp.concatenate([count, count], axis=1) > 0
            slotrows[r, :] = jnp.where(some, new, old).astype(BF16)
            return 0

        lax.fori_loop(0, 2, update, 0)

    def spread_rows(m):
        r = pl.ds(pl.multiple_of(m * 256, 256), 256)
        mask = keyline[...] == (iota((256, 512), 0) + m * 256).astype(F32)
        hit = jnp.sum(jnp.where(mask, 1.0, 0.0), axis=1, keepdims=True)
        fresh[r, :] = jnp.where(hit > 0, dot(onehot(mask), slotrows[...]), mem[r, cols].astype(F32)).astype(BF16)

    def tick(i, _):
        @pl.when(i < PLANE)
        def _():
            step_b(i)

        @pl.when((i + AHEAD < PLANE) & (i % 2 == 0))
        def _():
            step_a((i + AHEAD) // 2)

        @pl.when(i == TICK_SELF)
        def _():
            do_self()

        @pl.when(i == TICK_BACK)
        def _():
            do_back()

        @pl.when((i >= LAG_C) & (i < PLANE + LAG_C))
        def _():
            step_c(i - LAG_C)

        @pl.when((i > LAG_D) & ((i - LAG_D) % 2 == 1))
        def _():
            step_d((i - LAG_D - 1) // 2)

        @pl.when(i == TICK_GRU)
        def _():
            do_share()

        @pl.when((i >= TICK_GRU) & (i < TICK_GRU + GRU_TICKS))
        def _():
            def tile(n, _):
                spread_rows((i - TICK_GRU) * GRU_TILES + n)
                return 0

            lax.fori_loop(0, GRU_TILES, tile, 0)

        return 0

    lax.fori_loop(0, TICKS, tick, 0)
    fresh_cp = pltpu.make_async_copy(fresh, mem_out, tailsem.at[2])
    fresh_cp.start()

    same = (iota((128, 256), 0) % 16) == (iota((128, 256), 1) // 16)
    headcol = iota((16, W), 1) // (W // HEADS)

    def attend(t, _):
        r = pl.ds(pl.multiple_of(t * 512, 512), 512)
        nb = jnp.concatenate([acc[r, :], te[r, :]], axis=1)
        keys = dot(nb, wk[...]).astype(BF16)
        vals = dot(nb, wv[...]).astype(BF16)
        for u in range(2):
            k = keys[256 * u : 256 * u + 256]
            score = lax.dot_general(qm[2 * t + u], k, (((1,), (1,)), ((), ())), preferred_element_type=F32) * 0.125
            expo = jnp.where(same, jnp.exp(score), 0.0)
            weights = (expo / jnp.sum(expo, axis=1, keepdims=True)).astype(BF16)
            full = dot(weights, vals[256 * u : 256 * u + 256])
            out = jnp.zeros((16, W), F32)
            for h in range(HEADS):
                out = jnp.where(headcol == h, full[16 * h : 16 * h + 16], out)
            att[pl.ds(pl.multiple_of(t * 32 + 16 * u, 16), 16), :] = out.astype(BF16)
        return 0

    lax.fori_loop(0, 4, attend, 0)
    mine128 = pl.ds(pl.multiple_of(c * 128, 128), 128)
    emb[mine128, :] = (dot(att[...], wo[...]) + ebase[...]).astype(BF16)
    send = remote(emb.at[mine128], emb.at[mine128], tailsem.at[0], tailsem.at[1], sib)
    send.start()

    def drain(g, _):
        wait(pk.at[g, pl.ds(0, 112)], s1s.at[g])

        @pl.when(g < PLANE - 1)
        def _():
            wait(r1.at[g], s2s.at[g])

        wait(r1.at[g], sbs.at[g])
        return 0

    lax.fori_loop(0, PLANE, drain, 0)
    wait(sp.at[c, pl.ds(0, 224)], selfsem.at[0])
    wait(sp2.at[pl.ds(0, 240)], selfsem.at[2])
    wait(st.at[c], selfsem.at[4])
    wait(mb.at[pl.ds(0, 240)], backsem.at[0])
    wait(mp2.at[pl.ds(0, 224)], backsem.at[2])
    wait(mu.at[c], backsem.at[4])
    send.wait()
    emb_cp = pltpu.make_async_copy(emb, emb_out, tailsem.at[3])
    emb_cp.start()
    fresh_cp.wait()
    emb_cp.wait()


def deliver(emb, fresh, emb_out, mem_out, ebuf, epair, buf, load, store):
    parts = [pl.ds(ROWS // 2 * n, ROWS // 2) for n in range(2)]
    loads = [pltpu.make_async_copy(fresh.at[r], buf.at[r], load.at[n]) for n, r in enumerate(parts)]
    stores = [pltpu.make_async_copy(buf.at[r], mem_out.at[r], store.at[n]) for n, r in enumerate(parts)]
    first = pltpu.make_async_copy(emb, ebuf, load.at[2])
    first.start()
    for cp in loads:
        cp.start()
    first.wait()
    for n in range(2):
        epair[:, n, :] = ebuf[pl.ds(128 * n, 128), :]
    last = pltpu.make_async_copy(epair, emb_out, store.at[2])
    for n in range(2):
        loads[n].wait()
        stores[n].start()
    last.start()
    for cp in stores:
        cp.wait()
    last.wait()


def per_device(
    memory, ev_time, nbr_time, edge_feat, self_slot, nbr_slot, serve_self, serve_rows, freq, phase,
    w_query, w_key, w_value, w_out, w_self, w_msg_self, w_msg_other, w_msg_time, w_msg_edge, w_in, w_hid,
):
    vmem = pl.BlockSpec(memory_space=pltpu.VMEM)
    hbm = pl.BlockSpec(memory_space=pl.ANY)
    v = lambda *s: pltpu.VMEM(s, BF16)
    vf = lambda *s: pltpu.VMEM(s, F32)
    dma = lambda n: pltpu.SemaphoreType.DMA((n,))
    emb, fresh = pl.pallas_call(
        kernel,
        out_shape=(jax.ShapeDtypeStruct((256, W), BF16), jax.ShapeDtypeStruct((ROWS, HALF), BF16)),
        in_specs=[vmem] * 8 + [hbm] * 13,
        out_specs=(hbm, hbm),
        scratch_shapes=[
            v(ROWS, W), v(640, W), v(640, W), v(640, W), v(W, W), v(W, W), v(W, W), v(W, W), v(128, W), v(128, W),
            v(2, 64, 128), v(3, W, HALF), v(3, W, HALF),
            vf(128, 128), vf(128, 128), vf(128, 128), vf(2, 256, 128),
            v(16, 128, W), v(16, 128, W), v(2, 16, 128, W), v(2048, W), vf(2048, 128), v(2048, 128),
            v(2, 256, W), v(256, W), v(256, W), v(2, 256, W), v(256, MSGW), v(256, MSGW), v(256, MSGW), v(2, 256, MSGW),
            v(256, W), v(8, 128, W), vf(128, W), v(128, W), v(256, W), v(ROWS, HALF), vf(4, 128), vf(1, 512), vf(3, 512, HALF), v(512, HALF),
            dma(3), dma(10), dma(10), dma(10), dma(16), dma(16), dma(16), dma(16), dma(16), dma(16),
            dma(6), dma(6), dma(4),
        ],
        compiler_params=pltpu.CompilerParams(
            collective_id=0, has_side_effects=True, vmem_limit_bytes=60 * 1024 * 1024
        ),
    )(
        ev_time.reshape(1, 128), nbr_time.transpose(1, 2, 0), nbr_slot.transpose(1, 2, 0), self_slot.T,
        serve_self[0].T, serve_rows[0].T, freq.reshape(1, 128), phase.reshape(1, 128), memory, edge_feat.T,
        w_query, w_key, w_value, w_out, w_self,
        w_msg_self, w_msg_other, w_msg_time, w_msg_edge, w_in.transpose(1, 0, 2), w_hid.transpose(1, 0, 2),
    )
    return pl.pallas_call(
        deliver,
        out_shape=(jax.ShapeDtypeStruct((128, 2, W), BF16), jax.ShapeDtypeStruct((ROWS, HALF), BF16)),
        in_specs=[hbm, hbm],
        out_specs=(hbm, hbm),
        scratch_shapes=[v(256, W), v(128, 2, W), v(ROWS, HALF), dma(3), dma(3)],
    )(emb, fresh)


def solution(mesh):
    return jax.shard_map(
        per_device,
        mesh=mesh,
        in_specs=(
            P("nodes", None), P("nodes"), P("nodes", None, None), P("nodes", "mp"), P("nodes", None),
            P("nodes", None, None), P("nodes", None, None), P("nodes", None, None), P(), P(),
            P(None, "mp"), P(None, "mp"), P(None, "mp"), P("mp", None), P("mp", None), P("mp", None),
            P("mp", None), P("mp", None), P("mp", None), P(None, None, "mp"), P(None, None, "mp"),
        ),
        out_specs=(P("nodes", None, None), P("nodes", "mp")),
        check_vma=False,
    )
```

```python
import functools

import jax
import jax.numpy as jnp
from jax import lax
from jax.experimental import pallas as pl
from jax.experimental.pallas import tpu as pltpu
from jax.sharding import PartitionSpec as P

MESH = pl.DeviceIdType.MESH
F32 = jnp.float32
BF16 = jnp.bfloat16
HEADS = 8
X, Y, Z = 4, 4, 8
PLANE = X * Y
W = 512
ROWS = 2048
HALF = W // 2
MSGW = W + 128
DZ_ORDER = (4, 3, 5, 2, 6, 1, 7)
AHEAD = 4
LAG_C, LAG_D = 2, 3
TICKS = PLANE + LAG_D
TICK_SELF, TICK_BACK = 2, 11


def dot(a, b):
    return jnp.dot(a, b, preferred_element_type=F32)


def iota(shape, dim):
    return lax.broadcasted_iota(jnp.int32, shape, dim)


def onehot(mask):
    return jnp.where(mask, 1.0, 0.0).astype(BF16)


def cosine(angle):
    turns = jnp.floor(angle * 0.15915494309189535 + 0.5)
    r = angle - turns * 6.28125
    r = r - turns * 0.0019353071795864769
    h = 0.5 * r
    s = h * h
    poly = 1.6059043836821613e-10
    for coef in (
        -2.5052108385441720e-08,
        2.7557319223985893e-06,
        -1.9841269841269841e-04,
        8.3333333333333333e-03,
        -1.6666666666666666e-01,
        1.0,
    ):
        poly = poly * s + coef
    sine = poly * h
    return 1.0 - 2.0 * sine * sine


def kernel(
    ev, nbt, nslot, sslot, sself, srows, freq, phase, memory, edge, wq_h, wk_h, wv_h, wo_h, ws_h, wms_h, wmo_h, wmt_h, wme_h, win_h, whid_h,
    emb_out, rows_out, key_out,
    mem, wq, wk, wv, wo, ws, wms, wmo, wmt, wme, edges, win, whid,
    picks, nbrs, dts, serve, pk, r1, tab, acc, tcol, te, sp, sr1, sp2, st, mb, mr1, mp2, mu, selfs, qm, ebase, att, emb, hits, lines, keyline, ghs, slotrows,
    in_sem, wl, wsd, wrc, s1s, s1r, s2s, s2r, sbs, sbr, selfsem, backsem, tailsem,
):
    me = lax.axis_index("nodes")
    c = lax.axis_index("mp")
    x, y, z = me // (Y * Z), (me // Z) % Y, me % Z
    p = me // Z
    sib = (me, 1 - c)

    def plane(k, sign):
        dx, dy = k // Y, k % Y
        return ((x + X + sign * dx) % X) * Y + (y + Y + sign * dy) % Y

    def to(g):
        return plane((g + 1) % PLANE, 1 - 2 * c)

    def frm(g, core):
        return plane((g + 1) % PLANE, 2 * core - 1)

    def zpeer(dz):
        return (z + dz) % Z

    def zdev(dz):
        return (p * Z + zpeer(dz), c)

    def remote(src, dst, s, r, dev):
        return pltpu.make_async_remote_copy(src, dst, s, r, device_id=dev, device_id_type=MESH)

    def wait(ref, sem):
        pltpu.make_async_copy(ref, ref, sem).wait()

    mem_cp = pltpu.make_async_copy(memory, mem, in_sem.at[0])
    mem_cp.start()
    cols = pl.ds(pl.multiple_of(c * HALF, HALF), HALF)
    rows256 = pl.ds(pl.multiple_of(c * HALF, HALF), HALF)
    rows64 = pl.ds(pl.multiple_of(c * 64, 64), 64)
    shared = [
        (wms_h, wms.at[rows256]), (wmo_h, wmo.at[rows256]), (wmt_h, wmt.at[rows64]), (wme_h, wme.at[rows64]),
        (edge, edges.at[c]), (wq_h, wq.at[:, cols]), (ws_h, ws.at[rows256]), (wk_h, wk.at[:, cols]),
        (wv_h, wv.at[:, cols]), (wo_h, wo.at[rows256]),
    ]
    win_cp = pltpu.make_async_copy(win_h, win, in_sem.at[1])
    whid_cp = pltpu.make_async_copy(whid_h, whid, in_sem.at[2])

    bar = pltpu.get_barrier_semaphore()
    pl.semaphore_signal(bar, inc=1, device_id=sib, device_id_type=MESH)
    for dz in DZ_ORDER:
        pl.semaphore_signal(bar, inc=1, device_id=zdev(dz), device_id_type=MESH)

    def greet(k, _):
        pl.semaphore_signal(bar, inc=1, device_id=(plane(k, 1) * Z + z, c), device_id_type=MESH)
        return 0

    lax.fori_loop(1, PLANE, greet, 0)
    for n, (src, dst) in enumerate(shared):
        pltpu.make_async_copy(src, dst, wl.at[n]).start()
    win_cp.start()
    whid_cp.start()

    def turn(rows):
        full = jnp.concatenate([rows, jnp.zeros((128 - rows.shape[0], 128), jnp.int32)], axis=0)
        return jnp.transpose(full.astype(F32))

    def spread(block, first):
        n = block.shape[0] * 16
        many = jnp.broadcast_to(block[:, None, :], (block.shape[0], 16, 128)).reshape(n, 128)
        take = iota((n, 128), 1) == first + iota((n, 128), 0) % 16
        return jnp.sum(jnp.where(take, many, 0.0), axis=1, keepdims=True)

    def column(line):
        return jnp.transpose(jnp.broadcast_to(line.astype(F32), (128, 128)))

    lanes2048 = iota((1, ROWS), 1).astype(F32)

    def pick(col):
        return dot(onehot(col == lanes2048), mem[...]).astype(BF16)

    picks[...] = turn(srows[...])
    by_node = turn(sself[...])
    high = jnp.floor(by_node * 0.0625)
    parts = jnp.concatenate([high, by_node - 16.0 * high], axis=1).astype(BF16)
    si, sj = iota((256, 128), 0), iota((256, 128), 1)
    node = ((si // 2) % PLANE) * Z + si // 32
    both = dot(onehot(sj == node), parts)
    both = 16.0 * both[:, 0:128] + both[:, 128:256]
    for core in range(2):
        col = jnp.sum(jnp.where(sj == 2 * core + si % 2, both, 0.0), axis=1, keepdims=True)
        wide = jnp.broadcast_to(col, (256, 128))
        serve[core] = wide
        for n in range(2):
            lines[pl.ds(2 * core + n, 1), :] = jnp.transpose(wide[128 * n : 128 * n + 128])[0:1]
    mem_cp.wait()

    def pick_self(core, _):
        sp[core] = pick(serve[core, :, pl.ds(0, 1)])
        return 0

    pick_self(c, 0)
    own32 = pl.ds(pl.multiple_of(z * 32, 32), 32)
    own16 = pl.ds(pl.multiple_of(z * 16, 16), 16)
    plane16 = pl.ds(pl.multiple_of(p * 16, 16), 16)
    sr1[own32, :] = sp[c, own32, :]
    pl.semaphore_wait(bar, Z - 1 + PLANE - 1 + 1)
    for dz in DZ_ORDER:
        blk = pl.ds(pl.multiple_of(zpeer(dz) * 32, 32), 32)
        remote(sp.at[c, blk], sr1.at[own32], selfsem.at[0], selfsem.at[1], zdev(dz)).start()
    for n, (src, dst) in enumerate(shared):
        remote(src, dst, wsd.at[n], wrc.at[n], sib).start()

    def step_a(j):
        rows = [picks[pl.ds(pl.multiple_of(to(2 * j + n) * Z, Z), Z), :] for n in range(2)]
        got = pick(spread(jnp.concatenate(rows, axis=0), 16 * c))
        for n in range(2):
            g = 2 * j + n
            pk[g] = got[128 * n : 128 * n + 128]
        for n in range(2):
            g = 2 * j + n
            r1[g, own16, :] = pk[g, own16, :]
            for dz in DZ_ORDER:
                blk = pl.ds(pl.multiple_of(zpeer(dz) * 16, 16), 16)
                remote(pk.at[g, blk], r1.at[g, own16], s1s.at[g], s1r.at[g], zdev(dz)).start()

    def step_b(g):
        wait(r1.at[g, pl.ds(0, 112)], s1r.at[g])

        @pl.when(g < PLANE - 1)
        def _():
            remote(r1.at[g], tab.at[c, p], s2s.at[g], s2r.at[g], (to(g) * Z + z, c)).start()

        @pl.when(g == PLANE - 1)
        def _():
            remote(r1.at[g], tab.at[c, p], sbs.at[g], sbr.at[g], sib).start()
            pltpu.make_async_copy(r1.at[g], tab.at[c, p], s2r.at[g]).start()

    def step_c(g):
        part = tab.at[c, frm(g, c)]
        wait(part, s2r.at[g])

        @pl.when(g < PLANE - 1)
        def _():
            remote(part, part, sbs.at[g], sbr.at[g], sib).start()

    lanes128 = iota((1, 128), 1).astype(F32)

    def step_d(j):
        tables, marks = [], []
        for n in range(2):
            g = 2 * j + n
            wait(tab.at[1 - c, frm(g, 1 - c)], sbr.at[g])
        for n in range(2):
            for core in range(2):
                src = frm(2 * j + n, core)
                tables.append(tab[core, src])
                marks.append(lanes128 + (src * 128 + core * ROWS).astype(F32))
        table = jnp.concatenate(tables, axis=0)

        def tile(m, _):
            r = pl.ds(pl.multiple_of(m * 512, 512), 512)
            at = tcol[r, :]
            oh = jnp.concatenate([onehot(at == mark) for mark in marks], axis=1)
            acc[r, :] = acc[r, :] + dot(oh, table).astype(BF16)
            return 0

        lax.fori_loop(0, 4, tile, 0)

    def first(g, _):
        step_a(g)
        return 0

    lax.fori_loop(0, AHEAD // 2, first, 0)
    pick_self(1 - c, 0)

    slot = nslot[c]
    nbrs[...] = turn((slot % 32 // 16) * ROWS + (slot // 32) * 16 + slot % 16)
    dts[...] = turn(ev[...] - nbt[c])

    def prepare(b, _):
        r = pl.ds(pl.multiple_of(b * 256, 256), 256)
        e = pl.ds(pl.multiple_of(b * 16, 16), 16)
        tcol[r, :] = jnp.broadcast_to(spread(nbrs[e, :], 0), (256, 128))
        te[r, :] = cosine(spread(dts[e, :], 0) * freq[...] + phase[...]).astype(BF16)
        acc[r, :] = jnp.zeros((256, W), BF16)
        return 0

    lax.fori_loop(0, 8, prepare, 0)

    wait(sr1.at[pl.ds(0, 224)], selfsem.at[1])
    out_i, in_j = iota((256, 256), 0), iota((256, 256), 1)
    to_plane = onehot(in_j == ((out_i // 2) % Z) * 32 + (out_i // 16) * 2 + out_i % 2)
    sp2[...] = dot(to_plane, sr1[...]).astype(BF16)
    st[c, plane16, :] = sp2[plane16, :]

    def self_plane(k, _):
        q = plane(k, 1)
        blk = pl.ds(pl.multiple_of(q * 16, 16), 16)
        remote(sp2.at[blk], st.at[c, plane16], selfsem.at[2], selfsem.at[3], (q * Z + z, c)).start()
        return 0

    lax.fori_loop(1, PLANE, self_plane, 0)
    whid_cp.wait()

    def hidden(n, _):
        for g in range(3):
            ghs[g, pl.ds(pl.multiple_of(n * 256, 256), 256), :] = dot(sp[n], whid[g])
        return 0

    lax.fori_loop(0, 2, hidden, 0)

    def do_self():
        wait(st.at[c, pl.ds(0, 240)], selfsem.at[3])
        remote(st.at[c], st.at[c], selfsem.at[4], selfsem.at[5], sib).start()
        for n, (src, dst) in enumerate(shared):
            pltpu.make_async_copy(src, dst, wl.at[n]).wait()
            remote(src, dst, wsd.at[n], wrc.at[n], sib).wait()
        wait(st.at[1 - c], selfsem.at[5])
        table = jnp.concatenate([st[0], st[1]], axis=0)
        lanes512 = iota((128, W), 1).astype(F32)

        ends = (sslot[...] % 4 // 2) * 256 + (sslot[...] // 4) * 2 + sslot[...] % 2
        for n in range(2):
            at = jnp.tile(column(ends[n : n + 1]), (1, 4))
            selfs[pl.ds(128 * n, 128), :] = dot(onehot(at == lanes512), table).astype(BF16)
        mine = selfs[...]
        other = jnp.concatenate([mine[128:256], mine[0:128]], axis=0)
        te_m = jnp.concatenate(
            [cosine(column(ev[...] - nbt[n, 0:1]) * freq[...] + phase[...]).astype(BF16) for n in range(2)], axis=0
        )
        msg = dot(mine, wms[...]) + dot(other, wmo[...]) + dot(te_m, wmt[...])
        feats = jnp.concatenate([edges[0], edges[1]], axis=0)
        shared_part = lax.dot_general(feats, wme[...], (((0,), (0,)), ((), ())), preferred_element_type=F32)
        msg = msg + jnp.concatenate([shared_part, shared_part], axis=0)
        slots = jnp.concatenate([ends[0:1], ends[1:2]], axis=1)
        member = onehot(jnp.broadcast_to(slots, (256, 256)) == out_i + c * 256)
        high = msg.astype(BF16)
        low = (msg - high.astype(F32)).astype(BF16)
        mb[:, pl.ds(0, W)] = (dot(member, high) + dot(member, low)).astype(BF16)
        mb[:, pl.ds(W, 128)] = dot(member, jnp.ones((256, 128), BF16)).astype(BF16)
        mr1[plane16, :] = mb[plane16, :]

        def back_plane(k, _):
            q = plane(k, 1)
            blk = pl.ds(pl.multiple_of(q * 16, 16), 16)
            remote(mb.at[blk], mr1.at[plane16], backsem.at[0], backsem.at[1], (q * Z + z, c)).start()
            return 0

        lax.fori_loop(1, PLANE, back_plane, 0)
        ours = selfs[pl.ds(pl.multiple_of(c * 128, 128), 128), :]
        te_s = jnp.broadcast_to(cosine(phase[...]).astype(BF16), (8, 128))
        query = (dot(ours, wq[pl.ds(0, W), :]) + dot(te_s, wq[pl.ds(W, 128), :])[0:1]).astype(BF16)
        ebase[...] = dot(ours, ws[...])
        head = iota((16, W), 1) // (W // HEADS)
        for t in range(8):
            part = query[16 * t : 16 * t + 16]
            for h in range(HEADS):
                qm[t, pl.ds(16 * h, 16), :] = jnp.where(head == h, part, jnp.zeros_like(part))

    def do_back():
        wait(mr1.at[pl.ds(0, 240)], backsem.at[1])
        to_z = onehot(in_j == ((out_i // 2) % PLANE) * 16 + (out_i // 32) * 2 + out_i % 2)
        mp2[...] = dot(to_z, mr1[...]).astype(BF16)
        mu[c, own32, :] = mp2[own32, :]
        for dz in DZ_ORDER:
            blk = pl.ds(pl.multiple_of(zpeer(dz) * 32, 32), 32)
            remote(mp2.at[blk], mu.at[c, own32], backsem.at[2], backsem.at[3], zdev(dz)).start()

    def do_marks():
        win_cp.wait()
        line = jnp.concatenate([lines[pl.ds(n, 1), :] for n in range(4)], axis=1)
        col = jnp.concatenate([serve[0], serve[1]], axis=0)
        same = jnp.tile(col, (1, 4)) == line
        hits[...] = onehot(same)
        before = same & (iota((512, 512), 0) < iota((512, 512), 1))
        rank = jnp.sum(jnp.where(before, 1.0, 0.0), axis=0, keepdims=True)
        keyline[...] = jnp.where(rank == 0.0, line, -1.0)

    def do_share():
        wait(mu.at[c, pl.ds(0, 224)], backsem.at[3])
        remote(mu.at[c], mu.at[c], backsem.at[4], backsem.at[5], sib).start()
        wait(mu.at[1 - c], backsem.at[5])

        def update(n, _):
            r = pl.ds(pl.multiple_of(n * 256, 256), 256)
            sums = dot(hits[r, :], jnp.concatenate([mu[0], mu[1]], axis=0))
            count = sums[:, W : W + 128]
            most = jnp.maximum(count, 1.0)
            mean = jnp.concatenate([sums[:, 128 * k : 128 * k + 128] / most for k in range(4)], axis=1).astype(BF16)
            gi = [dot(mean, win[g]) for g in range(3)]
            gh = [ghs[g, r, :] for g in range(3)]
            reset = jax.nn.sigmoid(gi[0] + gh[0])
            gate = jax.nn.sigmoid(gi[1] + gh[1])
            cand = jnp.tanh(gi[2] + reset * gh[2])
            old = sp[n, :, cols].astype(F32)
            new = (1.0 - gate) * cand + gate * old
            some = jnp.concatenate([count, count], axis=1) > 0
            slotrows[r, :] = jnp.where(some, new, old).astype(BF16)
            return 0

        lax.fori_loop(0, 2, update, 0)

    def tick(i, _):
        @pl.when(i < PLANE)
        def _():
            step_b(i)

        @pl.when((i + AHEAD < PLANE) & (i % 2 == 0))
        def _():
            step_a((i + AHEAD) // 2)

        @pl.when(i == TICK_SELF)
        def _():
            do_self()

        @pl.when(i == TICK_BACK)
        def _():
            do_back()
            do_marks()

        @pl.when((i >= LAG_C) & (i < PLANE + LAG_C))
        def _():
            step_c(i - LAG_C)

        @pl.when((i > LAG_D) & ((i - LAG_D) % 2 == 1))
        def _():
            step_d((i - LAG_D - 1) // 2)

        return 0

    lax.fori_loop(0, TICKS, tick, 0)

    same = (iota((128, 256), 0) % 16) == (iota((128, 256), 1) // 16)
    headcol = iota((16, W), 1) // (W // HEADS)

    def attend(t, _):
        r = pl.ds(pl.multiple_of(t * 512, 512), 512)
        nb = jnp.concatenate([acc[r, :], te[r, :]], axis=1)
        keys = dot(nb, wk[...]).astype(BF16)
        vals = dot(nb, wv[...]).astype(BF16)
        for u in range(2):
            k = keys[256 * u : 256 * u + 256]
            score = lax.dot_general(qm[2 * t + u], k, (((1,), (1,)), ((), ())), preferred_element_type=F32) * 0.125
            expo = jnp.where(same, jnp.exp(score), 0.0)
            weights = (expo / jnp.sum(expo, axis=1, keepdims=True)).astype(BF16)
            full = dot(weights, vals[256 * u : 256 * u + 256])
            out = jnp.zeros((16, W), F32)
            for h in range(HEADS):
                out = jnp.where(headcol == h, full[16 * h : 16 * h + 16], out)
            att[pl.ds(pl.multiple_of(t * 32 + 16 * u, 16), 16), :] = out.astype(BF16)
        return 0

    lax.fori_loop(0, 4, attend, 0)
    mine128 = pl.ds(pl.multiple_of(c * 128, 128), 128)
    emb[mine128, :] = (dot(att[...], wo[...]) + ebase[...]).astype(BF16)
    send = remote(emb.at[mine128], emb.at[mine128], tailsem.at[0], tailsem.at[1], sib)
    send.start()
    do_share()
    rows_cp = pltpu.make_async_copy(slotrows, rows_out, tailsem.at[2])
    rows_cp.start()
    key_cp = pltpu.make_async_copy(keyline, key_out, tailsem.at[4])
    key_cp.start()

    def drain(g, _):
        wait(pk.at[g, pl.ds(0, 112)], s1s.at[g])

        @pl.when(g < PLANE - 1)
        def _():
            wait(r1.at[g], s2s.at[g])

        wait(r1.at[g], sbs.at[g])
        return 0

    lax.fori_loop(0, PLANE, drain, 0)
    wait(sp.at[c, pl.ds(0, 224)], selfsem.at[0])
    wait(sp2.at[pl.ds(0, 240)], selfsem.at[2])
    wait(st.at[c], selfsem.at[4])
    wait(mb.at[pl.ds(0, 240)], backsem.at[0])
    wait(mp2.at[pl.ds(0, 224)], backsem.at[2])
    wait(mu.at[c], backsem.at[4])
    send.wait()
    emb_cp = pltpu.make_async_copy(emb, emb_out, tailsem.at[3])
    emb_cp.start()
    rows_cp.wait()
    key_cp.wait()
    emb_cp.wait()


def deliver(emb, rows, key, memory, emb_out, mem_out, ebuf, epair, rbuf, kbuf, old, new, load, store):
    c = lax.axis_index("mp")
    cols = pl.ds(pl.multiple_of(c * HALF, HALF), HALF)
    tiles = [pl.ds(512 * n, 512) for n in range(4)]
    olds = [pltpu.make_async_copy(memory.at[r, cols], old.at[r], load.at[n]) for n, r in enumerate(tiles)]
    news = [pltpu.make_async_copy(new.at[r], mem_out.at[r], store.at[n]) for n, r in enumerate(tiles)]
    rest = [
        pltpu.make_async_copy(key, kbuf, load.at[4]),
        pltpu.make_async_copy(rows, rbuf, load.at[5]),
        pltpu.make_async_copy(emb, ebuf, load.at[6]),
    ]
    for cp in rest + olds:
        cp.start()
    for cp in rest:
        cp.wait()
    for n, r in enumerate(tiles):
        mask = kbuf[...] == (iota((512, 512), 0) + 512 * n).astype(F32)
        hit = jnp.sum(jnp.where(mask, 1.0, 0.0), axis=1, keepdims=True)
        put = dot(onehot(mask), rbuf[...])
        olds[n].wait()
        new[r, :] = jnp.where(hit > 0, put, old[r, :].astype(F32)).astype(BF16)
        news[n].start()
    for n in range(2):
        epair[:, n, :] = ebuf[pl.ds(128 * n, 128), :]
    last = pltpu.make_async_copy(epair, emb_out, store.at[4])
    last.start()
    for cp in news:
        cp.wait()
    last.wait()


def per_device(
    memory, ev_time, nbr_time, edge_feat, self_slot, nbr_slot, serve_self, serve_rows, freq, phase,
    w_query, w_key, w_value, w_out, w_self, w_msg_self, w_msg_other, w_msg_time, w_msg_edge, w_in, w_hid,
):
    vmem = pl.BlockSpec(memory_space=pltpu.VMEM)
    hbm = pl.BlockSpec(memory_space=pl.ANY)
    v = lambda *s: pltpu.VMEM(s, BF16)
    vf = lambda *s: pltpu.VMEM(s, F32)
    dma = lambda n: pltpu.SemaphoreType.DMA((n,))
    emb, rows, key = pl.pallas_call(
        kernel,
        out_shape=(
            jax.ShapeDtypeStruct((256, W), BF16), jax.ShapeDtypeStruct((512, HALF), BF16),
            jax.ShapeDtypeStruct((1, 512), F32),
        ),
        in_specs=[vmem] * 8 + [hbm] * 13,
        out_specs=(hbm, hbm, hbm),
        scratch_shapes=[
            v(ROWS, W), v(640, W), v(640, W), v(640, W), v(W, W), v(W, W), v(W, W), v(W, W), v(128, W), v(128, W),
            v(2, 64, 128), v(3, W, HALF), v(3, W, HALF),
            vf(128, 128), vf(128, 128), vf(128, 128), vf(2, 256, 128),
            v(16, 128, W), v(16, 128, W), v(2, 16, 128, W), v(2048, W), vf(2048, 128), v(2048, 128),
            v(2, 256, W), v(256, W), v(256, W), v(2, 256, W), v(256, MSGW), v(256, MSGW), v(256, MSGW), v(2, 256, MSGW),
            v(256, W), v(8, 128, W), vf(128, W), v(128, W), v(256, W), v(W, W), vf(4, 128), vf(1, 512), vf(3, 512, HALF), v(512, HALF),
            dma(3), dma(10), dma(10), dma(10), dma(16), dma(16), dma(16), dma(16), dma(16), dma(16),
            dma(6), dma(6), dma(5),
        ],
        compiler_params=pltpu.CompilerParams(
            collective_id=0, has_side_effects=True, vmem_limit_bytes=60 * 1024 * 1024
        ),
    )(
        ev_time.reshape(1, 128), nbr_time.transpose(1, 2, 0), nbr_slot.transpose(1, 2, 0), self_slot.T,
        serve_self[0].T, serve_rows[0].T, freq.reshape(1, 128), phase.reshape(1, 128), memory, edge_feat.T,
        w_query, w_key, w_value, w_out, w_self,
        w_msg_self, w_msg_other, w_msg_time, w_msg_edge, w_in.transpose(1, 0, 2), w_hid.transpose(1, 0, 2),
    )
    return pl.pallas_call(
        deliver,
        out_shape=(jax.ShapeDtypeStruct((128, 2, W), BF16), jax.ShapeDtypeStruct((ROWS, HALF), BF16)),
        in_specs=[hbm] * 4,
        out_specs=(hbm, hbm),
        scratch_shapes=[
            v(256, W), v(128, 2, W), v(512, HALF), vf(1, 512), v(ROWS, HALF), v(ROWS, HALF), dma(7), dma(5),
        ],
    )(emb, rows, key, memory)


def solution(mesh):
    return jax.shard_map(
        per_device,
        mesh=mesh,
        in_specs=(
            P("nodes", None), P("nodes"), P("nodes", None, None), P("nodes", "mp"), P("nodes", None),
            P("nodes", None, None), P("nodes", None, None), P("nodes", None, None), P(), P(),
            P(None, "mp"), P(None, "mp"), P(None, "mp"), P("mp", None), P("mp", None), P("mp", None),
            P("mp", None), P("mp", None), P("mp", None), P(None, None, "mp"), P(None, None, "mp"),
        ),
        out_specs=(P("nodes", None, None), P("nodes", "mp")),
        check_vma=False,
    )
```

```python
import functools

import jax
import jax.numpy as jnp
from jax import lax
from jax.experimental import pallas as pl
from jax.experimental.pallas import tpu as pltpu
from jax.sharding import PartitionSpec as P

MESH = pl.DeviceIdType.MESH
F32 = jnp.float32
BF16 = jnp.bfloat16
HEADS = 8
X, Y, Z = 4, 4, 8
PLANE = X * Y
W = 512
ROWS = 2048
HALF = W // 2
MSGW = W + 128
DZ_ORDER = (4, 3, 5, 2, 6, 1, 7)
AHEAD = 4
LAG_C, LAG_D = 2, 3
TICKS = PLANE + LAG_D
TICK_SELF, TICK_BACK = 2, 11


def dot(a, b):
    return jnp.dot(a, b, preferred_element_type=F32)


def iota(shape, dim):
    return lax.broadcasted_iota(jnp.int32, shape, dim)


def onehot(mask):
    return jnp.where(mask, 1.0, 0.0).astype(BF16)


def cosine(angle):
    turns = jnp.floor(angle * 0.15915494309189535 + 0.5)
    r = angle - turns * 6.28125
    r = r - turns * 0.0019353071795864769
    h = 0.5 * r
    s = h * h
    poly = 1.6059043836821613e-10
    for coef in (
        -2.5052108385441720e-08,
        2.7557319223985893e-06,
        -1.9841269841269841e-04,
        8.3333333333333333e-03,
        -1.6666666666666666e-01,
        1.0,
    ):
        poly = poly * s + coef
    sine = poly * h
    return 1.0 - 2.0 * sine * sine


def kernel(
    ev_h, nbt_h, nslot_h, sslot_h, sself_h, srows_h, freq_h, phase_h, memory, edge, wq_h, wk_h, wv_h, wo_h, ws_h, wms_h, wmo_h, wmt_h, wme_h, win_h, whid_h,
    emb_out, rows_out, key_out,
    mem, wq, wk, wv, wo, ws, wms, wmo, wmt, wme, edges, win, whid,
    picks, nbrs, dts, serve, pk, r1, tab, acc, tcol, te, sp, sr1, sp2, st, mb, mr1, mp2, mu, selfs, qm, ebase, att, emb, hits, lines, keyline, ghs, slotrows, tk, tv,
    ev, nbt, nslot, sslot, sself, srows, freq, phase,
    in_sem, wl, wsd, wrc, s1s, s1r, s2s, s2r, sbs, sbr, selfsem, backsem, tailsem,
):
    me = lax.axis_index("nodes")
    c = lax.axis_index("mp")
    x, y, z = me // (Y * Z), (me // Z) % Y, me % Z
    p = me // Z
    sib = (me, 1 - c)

    def plane(k, sign):
        dx, dy = k // Y, k % Y
        return ((x + X + sign * dx) % X) * Y + (y + Y + sign * dy) % Y

    def to(g):
        return plane(PLANE - 1 - g, 1 - 2 * c)

    def frm(g, core):
        return plane(PLANE - 1 - g, 2 * core - 1)

    def zpeer(dz):
        return (z + dz) % Z

    def zdev(dz):
        return (p * Z + zpeer(dz), c)

    def remote(src, dst, s, r, dev):
        return pltpu.make_async_remote_copy(src, dst, s, r, device_id=dev, device_id_type=MESH)

    def wait(ref, sem):
        pltpu.make_async_copy(ref, ref, sem).wait()

    mem_cp = pltpu.make_async_copy(memory, mem, in_sem.at[0])
    small = [
        pltpu.make_async_copy(src, dst, in_sem.at[3 + n])
        for n, (src, dst) in enumerate(
            [(sself_h, sself), (srows_h, srows), (ev_h, ev), (nbt_h, nbt), (nslot_h, nslot), (sslot_h, sslot),
             (freq_h, freq), (phase_h, phase)]
        )
    ]
    cols = pl.ds(pl.multiple_of(c * HALF, HALF), HALF)
    rows256 = pl.ds(pl.multiple_of(c * HALF, HALF), HALF)
    rows64 = pl.ds(pl.multiple_of(c * 64, 64), 64)
    shared = [
        (wms_h, wms.at[rows256]), (wmo_h, wmo.at[rows256]), (wmt_h, wmt.at[rows64]), (wme_h, wme.at[rows64]),
        (edge, edges.at[c]), (wq_h, wq.at[:, cols]), (ws_h, ws.at[rows256]), (wk_h, wk.at[:, cols]),
        (wv_h, wv.at[:, cols]), (wo_h, wo.at[rows256]),
    ]
    win_cp = pltpu.make_async_copy(win_h, win, in_sem.at[1])
    whid_cp = pltpu.make_async_copy(whid_h, whid, in_sem.at[2])

    bar = pltpu.get_barrier_semaphore()
    pl.semaphore_signal(bar, inc=1, device_id=sib, device_id_type=MESH)
    for dz in DZ_ORDER:
        pl.semaphore_signal(bar, inc=1, device_id=zdev(dz), device_id_type=MESH)

    def greet(k, _):
        pl.semaphore_signal(bar, inc=1, device_id=(plane(k, 1) * Z + z, c), device_id_type=MESH)
        return 0

    lax.fori_loop(1, PLANE, greet, 0)
    for cp in small[0:2] + [mem_cp] + small[2:]:
        cp.start()
    for n, (src, dst) in enumerate(shared):
        pltpu.make_async_copy(src, dst, wl.at[n]).start()
    win_cp.start()
    whid_cp.start()

    def turn(rows):
        full = jnp.concatenate([rows, jnp.zeros((128 - rows.shape[0], 128), jnp.int32)], axis=0)
        return jnp.transpose(full.astype(F32))

    def spread(block, first):
        n = block.shape[0] * 16
        many = jnp.broadcast_to(block[:, None, :], (block.shape[0], 16, 128)).reshape(n, 128)
        take = iota((n, 128), 1) == first + iota((n, 128), 0) % 16
        return jnp.sum(jnp.where(take, many, 0.0), axis=1, keepdims=True)

    def column(line):
        return jnp.transpose(jnp.broadcast_to(line.astype(F32), (128, 128)))

    lanes2048 = iota((1, ROWS), 1).astype(F32)

    def pick(col):
        return dot(onehot(col == lanes2048), mem[...]).astype(BF16)

    for cp in small:
        cp.wait()
    picks[...] = turn(srows[...])
    by_node = turn(sself[...])
    high = jnp.floor(by_node * 0.0625)
    parts = jnp.concatenate([high, by_node - 16.0 * high], axis=1).astype(BF16)
    si, sj = iota((256, 128), 0), iota((256, 128), 1)
    node = ((si // 2) % PLANE) * Z + si // 32
    both = dot(onehot(sj == node), parts)
    both = 16.0 * both[:, 0:128] + both[:, 128:256]
    for core in range(2):
        col = jnp.sum(jnp.where(sj == 2 * core + si % 2, both, 0.0), axis=1, keepdims=True)
        wide = jnp.broadcast_to(col, (256, 128))
        serve[core] = wide
        for n in range(2):
            lines[pl.ds(2 * core + n, 1), :] = jnp.transpose(wide[128 * n : 128 * n + 128])[0:1]
    mem_cp.wait()

    def pick_self(core, _):
        sp[core] = pick(serve[core, :, pl.ds(0, 1)])
        return 0

    pick_self(c, 0)
    own32 = pl.ds(pl.multiple_of(z * 32, 32), 32)
    own16 = pl.ds(pl.multiple_of(z * 16, 16), 16)
    plane16 = pl.ds(pl.multiple_of(p * 16, 16), 16)
    sr1[own32, :] = sp[c, own32, :]
    pl.semaphore_wait(bar, Z - 1 + PLANE - 1 + 1)
    for dz in DZ_ORDER:
        blk = pl.ds(pl.multiple_of(zpeer(dz) * 32, 32), 32)
        remote(sp.at[c, blk], sr1.at[own32], selfsem.at[0], selfsem.at[1], zdev(dz)).start()
    for n, (src, dst) in enumerate(shared):
        remote(src, dst, wsd.at[n], wrc.at[n], sib).start()

    def step_a(j):
        rows = [picks[pl.ds(pl.multiple_of(to(2 * j + n) * Z, Z), Z), :] for n in range(2)]
        got = pick(spread(jnp.concatenate(rows, axis=0), 16 * c))
        for n in range(2):
            g = 2 * j + n
            pk[g] = got[128 * n : 128 * n + 128]
        for n in range(2):
            g = 2 * j + n
            r1[g, own16, :] = pk[g, own16, :]
            for dz in DZ_ORDER:
                blk = pl.ds(pl.multiple_of(zpeer(dz) * 16, 16), 16)
                remote(pk.at[g, blk], r1.at[g, own16], s1s.at[g], s1r.at[g], zdev(dz)).start()

    def step_b(g):
        wait(r1.at[g, pl.ds(0, 112)], s1r.at[g])

        @pl.when(g < PLANE - 1)
        def _():
            remote(r1.at[g], tab.at[c, p], s2s.at[g], s2r.at[g], (to(g) * Z + z, c)).start()

        @pl.when(g == PLANE - 1)
        def _():
            remote(r1.at[g], tab.at[c, p], sbs.at[g], sbr.at[g], sib).start()
            pltpu.make_async_copy(r1.at[g], tab.at[c, p], s2r.at[g]).start()

    def step_c(g):
        part = tab.at[c, frm(g, c)]
        wait(part, s2r.at[g])

        @pl.when(g < PLANE - 1)
        def _():
            remote(part, part, sbs.at[g], sbr.at[g], sib).start()

    lanes128 = iota((1, 128), 1).astype(F32)

    def step_d(j):
        tables, marks = [], []
        for n in range(2):
            g = 2 * j + n
            wait(tab.at[1 - c, frm(g, 1 - c)], sbr.at[g])
        for n in range(2):
            for core in range(2):
                src = frm(2 * j + n, core)
                tables.append(tab[core, src])
                marks.append(lanes128 + (src * 128 + core * ROWS).astype(F32))
        table = jnp.concatenate(tables, axis=0)

        def tile(m, _):
            r = pl.ds(pl.multiple_of(m * 512, 512), 512)
            at = tcol[r, :]
            oh = jnp.concatenate([onehot(at == mark) for mark in marks], axis=1)
            acc[r, :] = acc[r, :] + dot(oh, table).astype(BF16)
            return 0

        lax.fori_loop(0, 4, tile, 0)

    def first(g, _):
        step_a(g)
        return 0

    lax.fori_loop(0, AHEAD // 2, first, 0)
    pick_self(1 - c, 0)

    slot = nslot[c]
    nbrs[...] = turn((slot % 32 // 16) * ROWS + (slot // 32) * 16 + slot % 16)
    dts[...] = turn(ev[...] - nbt[c])

    def prepare(b, _):
        r = pl.ds(pl.multiple_of(b * 256, 256), 256)
        e = pl.ds(pl.multiple_of(b * 16, 16), 16)
        tcol[r, :] = jnp.broadcast_to(spread(nbrs[e, :], 0), (256, 128))
        te[r, :] = cosine(spread(dts[e, :], 0) * freq[...] + phase[...]).astype(BF16)
        acc[r, :] = jnp.zeros((256, W), BF16)
        return 0

    lax.fori_loop(0, 8, prepare, 0)

    wait(sr1.at[pl.ds(0, 224)], selfsem.at[1])
    out_i, in_j = iota((256, 256), 0), iota((256, 256), 1)
    to_plane = onehot(in_j == ((out_i // 2) % Z) * 32 + (out_i // 16) * 2 + out_i % 2)
    sp2[...] = dot(to_plane, sr1[...]).astype(BF16)
    st[c, plane16, :] = sp2[plane16, :]

    def self_plane(k, _):
        q = plane(k, 1)
        blk = pl.ds(pl.multiple_of(q * 16, 16), 16)
        remote(sp2.at[blk], st.at[c, plane16], selfsem.at[2], selfsem.at[3], (q * Z + z, c)).start()
        return 0

    lax.fori_loop(1, PLANE, self_plane, 0)
    whid_cp.wait()

    def hidden(n, _):
        for g in range(3):
            ghs[g, pl.ds(pl.multiple_of(n * 256, 256), 256), :] = dot(sp[n], whid[g])
        return 0

    lax.fori_loop(0, 2, hidden, 0)

    def do_self():
        wait(st.at[c, pl.ds(0, 240)], selfsem.at[3])
        remote(st.at[c], st.at[c], selfsem.at[4], selfsem.at[5], sib).start()
        for n, (src, dst) in enumerate(shared):
            pltpu.make_async_copy(src, dst, wl.at[n]).wait()
            remote(src, dst, wsd.at[n], wrc.at[n], sib).wait()
        wait(st.at[1 - c], selfsem.at[5])
        table = jnp.concatenate([st[0], st[1]], axis=0)
        lanes512 = iota((128, W), 1).astype(F32)

        ends = (sslot[...] % 4 // 2) * 256 + (sslot[...] // 4) * 2 + sslot[...] % 2
        for n in range(2):
            at = jnp.tile(column(ends[n : n + 1]), (1, 4))
            selfs[pl.ds(128 * n, 128), :] = dot(onehot(at == lanes512), table).astype(BF16)
        mine = selfs[...]
        other = jnp.concatenate([mine[128:256], mine[0:128]], axis=0)
        te_m = jnp.concatenate(
            [cosine(column(ev[...] - nbt[n, 0:1]) * freq[...] + phase[...]).astype(BF16) for n in range(2)], axis=0
        )
        msg = dot(mine, wms[...]) + dot(other, wmo[...]) + dot(te_m, wmt[...])
        feats = jnp.concatenate([edges[0], edges[1]], axis=0)
        shared_part = lax.dot_general(feats, wme[...], (((0,), (0,)), ((), ())), preferred_element_type=F32)
        msg = msg + jnp.concatenate([shared_part, shared_part], axis=0)
        slots = jnp.concatenate([ends[0:1], ends[1:2]], axis=1)
        member = onehot(jnp.broadcast_to(slots, (256, 256)) == out_i + c * 256)
        high = msg.astype(BF16)
        low = (msg - high.astype(F32)).astype(BF16)
        mb[:, pl.ds(0, W)] = (dot(member, high) + dot(member, low)).astype(BF16)
        mb[:, pl.ds(W, 128)] = dot(member, jnp.ones((256, 128), BF16)).astype(BF16)
        mr1[plane16, :] = mb[plane16, :]

        def back_plane(k, _):
            q = plane(k, 1)
            blk = pl.ds(pl.multiple_of(q * 16, 16), 16)
            remote(mb.at[blk], mr1.at[plane16], backsem.at[0], backsem.at[1], (q * Z + z, c)).start()
            return 0

        lax.fori_loop(1, PLANE, back_plane, 0)
        ours = selfs[pl.ds(pl.multiple_of(c * 128, 128), 128), :]
        te_s = jnp.broadcast_to(cosine(phase[...]).astype(BF16), (8, 128))
        query = (dot(ours, wq[pl.ds(0, W), :]) + dot(te_s, wq[pl.ds(W, 128), :])[0:1]).astype(BF16)
        ebase[...] = dot(ours, ws[...])
        head = iota((16, W), 1) // (W // HEADS)
        for t in range(8):
            part = query[16 * t : 16 * t + 16]
            for h in range(HEADS):
                qm[t, pl.ds(16 * h, 16), :] = jnp.where(head == h, part, jnp.zeros_like(part))

    def do_back():
        wait(mr1.at[pl.ds(0, 240)], backsem.at[1])
        to_z = onehot(in_j == ((out_i // 2) % PLANE) * 16 + (out_i // 32) * 2 + out_i % 2)
        mp2[...] = dot(to_z, mr1[...]).astype(BF16)
        mu[c, own32, :] = mp2[own32, :]
        for dz in DZ_ORDER:
            blk = pl.ds(pl.multiple_of(zpeer(dz) * 32, 32), 32)
            remote(mp2.at[blk], mu.at[c, own32], backsem.at[2], backsem.at[3], zdev(dz)).start()

    def do_marks():
        win_cp.wait()
        line = jnp.concatenate([lines[pl.ds(n, 1), :] for n in range(4)], axis=1)
        col = jnp.concatenate([serve[0], serve[1]], axis=0)
        same = jnp.tile(col, (1, 4)) == line
        hits[...] = onehot(same)
        before = same & (iota((512, 512), 0) < iota((512, 512), 1))
        rank = jnp.sum(jnp.where(before, 1.0, 0.0), axis=0, keepdims=True)
        keyline[...] = jnp.where(rank == 0.0, line, -1.0)

    def share_messages():
        wait(mu.at[c, pl.ds(0, 224)], backsem.at[3])
        remote(mu.at[c], mu.at[c], backsem.at[4], backsem.at[5], sib).start()

    def do_share():
        wait(mu.at[1 - c], backsem.at[5])

        def update(n, _):
            r = pl.ds(pl.multiple_of(n * 256, 256), 256)
            sums = dot(hits[r, :], jnp.concatenate([mu[0], mu[1]], axis=0))
            count = sums[:, W : W + 128]
            most = jnp.maximum(count, 1.0)
            mean = jnp.concatenate([sums[:, 128 * k : 128 * k + 128] / most for k in range(4)], axis=1).astype(BF16)
            gi = [dot(mean, win[g]) for g in range(3)]
            gh = [ghs[g, r, :] for g in range(3)]
            reset = jax.nn.sigmoid(gi[0] + gh[0])
            gate = jax.nn.sigmoid(gi[1] + gh[1])
            cand = jnp.tanh(gi[2] + reset * gh[2])
            old = sp[n, :, cols].astype(F32)
            new = (1.0 - gate) * cand + gate * old
            some = jnp.concatenate([count, count], axis=1) > 0
            slotrows[r, :] = jnp.where(some, new, old).astype(BF16)
            return 0

        lax.fori_loop(0, 2, update, 0)

    def tick(i, _):
        @pl.when(i < PLANE)
        def _():
            step_b(i)

        @pl.when((i + AHEAD < PLANE) & (i % 2 == 0))
        def _():
            step_a((i + AHEAD) // 2)

        @pl.when(i == TICK_SELF)
        def _():
            do_self()

        @pl.when(i == TICK_BACK)
        def _():
            do_back()
            do_marks()

            def times(t, _):
                r = pl.ds(pl.multiple_of(t * 512, 512), 512)
                tk[r, :] = dot(te[r, :], wk[pl.ds(W, 128), :])
                tv[r, :] = dot(te[r, :], wv[pl.ds(W, 128), :])
                return 0

            lax.fori_loop(0, 4, times, 0)

        @pl.when((i >= LAG_C) & (i < PLANE + LAG_C))
        def _():
            step_c(i - LAG_C)

        @pl.when((i > LAG_D) & ((i - LAG_D) % 2 == 1))
        def _():
            step_d((i - LAG_D - 1) // 2)

        return 0

    lax.fori_loop(0, TICKS, tick, 0)

    same = (iota((128, 256), 0) % 16) == (iota((128, 256), 1) // 16)
    headcol = iota((16, W), 1) // (W // HEADS)

    def attend(t, _):
        r = pl.ds(pl.multiple_of(t * 512, 512), 512)
        nb = acc[r, :]
        keys = (dot(nb, wk[pl.ds(0, W), :]) + tk[r, :]).astype(BF16)
        vals = (dot(nb, wv[pl.ds(0, W), :]) + tv[r, :]).astype(BF16)

        @pl.when(t == 2)
        def _():
            share_messages()

        for u in range(2):
            k = keys[256 * u : 256 * u + 256]
            score = lax.dot_general(qm[2 * t + u], k, (((1,), (1,)), ((), ())), preferred_element_type=F32) * 0.125
            expo = jnp.where(same, jnp.exp(score), 0.0)
            weights = (expo / jnp.sum(expo, axis=1, keepdims=True)).astype(BF16)
            full = dot(weights, vals[256 * u : 256 * u + 256])
            out = jnp.zeros((16, W), F32)
            for h in range(HEADS):
                out = jnp.where(headcol == h, full[16 * h : 16 * h + 16], out)
            att[pl.ds(pl.multiple_of(t * 32 + 16 * u, 16), 16), :] = out.astype(BF16)
        return 0

    lax.fori_loop(0, 4, attend, 0)
    mine128 = pl.ds(pl.multiple_of(c * 128, 128), 128)
    emb[mine128, :] = (dot(att[...], wo[...]) + ebase[...]).astype(BF16)
    send = remote(emb.at[mine128], emb.at[mine128], tailsem.at[0], tailsem.at[1], sib)
    send.start()
    do_share()
    rows_cp = pltpu.make_async_copy(slotrows, rows_out, tailsem.at[2])
    rows_cp.start()
    key_cp = pltpu.make_async_copy(keyline, key_out, tailsem.at[4])
    key_cp.start()

    def drain(g, _):
        wait(pk.at[g, pl.ds(0, 112)], s1s.at[g])

        @pl.when(g < PLANE - 1)
        def _():
            wait(r1.at[g], s2s.at[g])

        wait(r1.at[g], sbs.at[g])
        return 0

    lax.fori_loop(0, PLANE, drain, 0)
    wait(sp.at[c, pl.ds(0, 224)], selfsem.at[0])
    wait(sp2.at[pl.ds(0, 240)], selfsem.at[2])
    wait(st.at[c], selfsem.at[4])
    wait(mb.at[pl.ds(0, 240)], backsem.at[0])
    wait(mp2.at[pl.ds(0, 224)], backsem.at[2])
    wait(mu.at[c], backsem.at[4])
    send.wait()
    emb_cp = pltpu.make_async_copy(emb, emb_out, tailsem.at[3])
    emb_cp.start()
    rows_cp.wait()
    key_cp.wait()
    emb_cp.wait()


def deliver(emb, rows, key, memory, emb_out, mem_out, ebuf, epair, rbuf, kbuf, old, new, load, store):
    c = lax.axis_index("mp")
    cols = pl.ds(pl.multiple_of(c * HALF, HALF), HALF)
    tiles = [pl.ds(512 * n, 512) for n in range(4)]
    olds = [pltpu.make_async_copy(memory.at[r, cols], old.at[r], load.at[n]) for n, r in enumerate(tiles)]
    news = [pltpu.make_async_copy(new.at[r], mem_out.at[r], store.at[n]) for n, r in enumerate(tiles)]
    rest = [
        pltpu.make_async_copy(key, kbuf, load.at[4]),
        pltpu.make_async_copy(rows, rbuf, load.at[5]),
        pltpu.make_async_copy(emb, ebuf, load.at[6]),
    ]
    for cp in rest + olds:
        cp.start()
    for cp in rest:
        cp.wait()
    for n, r in enumerate(tiles):
        mask = kbuf[...] == (iota((512, 512), 0) + 512 * n).astype(F32)
        hit = jnp.sum(jnp.where(mask, 1.0, 0.0), axis=1, keepdims=True)
        put = dot(onehot(mask), rbuf[...])
        olds[n].wait()
        new[r, :] = jnp.where(hit > 0, put, old[r, :].astype(F32)).astype(BF16)
        news[n].start()
    for n in range(2):
        epair[:, n, :] = ebuf[pl.ds(128 * n, 128), :]
    last = pltpu.make_async_copy(epair, emb_out, store.at[4])
    last.start()
    for cp in news:
        cp.wait()
    last.wait()


def per_device(
    memory, ev_time, nbr_time, edge_feat, self_slot, nbr_slot, serve_self, serve_rows, freq, phase,
    w_query, w_key, w_value, w_out, w_self, w_msg_self, w_msg_other, w_msg_time, w_msg_edge, w_in, w_hid,
):
    hbm = pl.BlockSpec(memory_space=pl.ANY)
    v = lambda *s: pltpu.VMEM(s, BF16)
    vf = lambda *s: pltpu.VMEM(s, F32)
    vi = lambda *s: pltpu.VMEM(s, jnp.int32)
    dma = lambda n: pltpu.SemaphoreType.DMA((n,))
    emb, rows, key = pl.pallas_call(
        kernel,
        out_shape=(
            jax.ShapeDtypeStruct((256, W), BF16), jax.ShapeDtypeStruct((512, HALF), BF16),
            jax.ShapeDtypeStruct((1, 512), F32),
        ),
        in_specs=[hbm] * 21,
        out_specs=(hbm, hbm, hbm),
        scratch_shapes=[
            v(ROWS, W), v(640, W), v(640, W), v(640, W), v(W, W), v(W, W), v(W, W), v(W, W), v(128, W), v(128, W),
            v(2, 64, 128), v(3, W, HALF), v(3, W, HALF),
            vf(128, 128), vf(128, 128), vf(128, 128), vf(2, 256, 128),
            v(16, 128, W), v(16, 128, W), v(2, 16, 128, W), v(2048, W), vf(2048, 128), v(2048, 128),
            v(2, 256, W), v(256, W), v(256, W), v(2, 256, W), v(256, MSGW), v(256, MSGW), v(256, MSGW), v(2, 256, MSGW),
            v(256, W), v(8, 128, W), vf(128, W), v(128, W), v(256, W), v(W, W), vf(4, 128), vf(1, 512), vf(3, 512, HALF), v(512, HALF), vf(2048, W), vf(2048, W),
            vi(1, 128), vi(2, 16, 128), vi(2, 16, 128), vi(2, 128), vi(4, 128), vi(32, 128), vf(1, 128), vf(1, 128),
            dma(11), dma(10), dma(10), dma(10), dma(16), dma(16), dma(16), dma(16), dma(16), dma(16),
            dma(6), dma(6), dma(5),
        ],
        compiler_params=pltpu.CompilerParams(
            collective_id=0, has_side_effects=True, vmem_limit_bytes=60 * 1024 * 1024
        ),
    )(
        ev_time.reshape(1, 128), nbr_time.transpose(1, 2, 0), nbr_slot.transpose(1, 2, 0), self_slot.T,
        serve_self[0].T, serve_rows[0].T, freq.reshape(1, 128), phase.reshape(1, 128), memory, edge_feat.T,
        w_query, w_key, w_value, w_out, w_self,
        w_msg_self, w_msg_other, w_msg_time, w_msg_edge, w_in.transpose(1, 0, 2), w_hid.transpose(1, 0, 2),
    )
    return pl.pallas_call(
        deliver,
        out_shape=(jax.ShapeDtypeStruct((128, 2, W), BF16), jax.ShapeDtypeStruct((ROWS, HALF), BF16)),
        in_specs=[hbm] * 4,
        out_specs=(hbm, hbm),
        scratch_shapes=[
            v(256, W), v(128, 2, W), v(512, HALF), vf(1, 512), v(ROWS, HALF), v(ROWS, HALF), dma(7), dma(5),
        ],
    )(emb, rows, key, memory)


def solution(mesh):
    return jax.shard_map(
        per_device,
        mesh=mesh,
        in_specs=(
            P("nodes", None), P("nodes"), P("nodes", None, None), P("nodes", "mp"), P("nodes", None),
            P("nodes", None, None), P("nodes", None, None), P("nodes", None, None), P(), P(),
            P(None, "mp"), P(None, "mp"), P(None, "mp"), P("mp", None), P("mp", None), P("mp", None),
            P("mp", None), P("mp", None), P("mp", None), P(None, None, "mp"), P(None, None, "mp"),
        ),
        out_specs=(P("nodes", None, None), P("nodes", "mp")),
        check_vma=False,
    )
```

```python
import functools

import jax
import jax.numpy as jnp
from jax import lax
from jax.experimental import pallas as pl
from jax.experimental.pallas import tpu as pltpu
from jax.sharding import PartitionSpec as P

MESH = pl.DeviceIdType.MESH
F32 = jnp.float32
BF16 = jnp.bfloat16
HEADS = 8
X, Y, Z = 4, 4, 8
PLANE = X * Y
W = 512
ROWS = 2048
HALF = W // 2
MSGW = W + 128
DZ_ORDER = (4, 3, 5, 2, 6, 1, 7)
AHEAD = 4
LAG_C, LAG_D = 2, 3
TICKS = PLANE + LAG_D
TICK_SELF, TICK_MARKS, TICK_BACK = 2, 8, 15


def dot(a, b):
    return jnp.dot(a, b, preferred_element_type=F32)


def iota(shape, dim):
    return lax.broadcasted_iota(jnp.int32, shape, dim)


def onehot(mask):
    return jnp.where(mask, 1.0, 0.0).astype(BF16)


def cosine(angle):
    turns = jnp.floor(angle * 0.15915494309189535 + 0.5)
    r = angle - turns * 6.28125
    r = r - turns * 0.0019353071795864769
    h = 0.5 * r
    s = h * h
    poly = 1.6059043836821613e-10
    for coef in (
        -2.5052108385441720e-08,
        2.7557319223985893e-06,
        -1.9841269841269841e-04,
        8.3333333333333333e-03,
        -1.6666666666666666e-01,
        1.0,
    ):
        poly = poly * s + coef
    sine = poly * h
    return 1.0 - 2.0 * sine * sine


def kernel(
    ev_h, nbt_h, nslot_h, sslot_h, sself_h, srows_h, freq_h, phase_h, memory, edge, wq_h, wk_h, wv_h, wo_h, ws_h, wms_h, wmo_h, wmt_h, wme_h, win_h, whid_h,
    emb_out, rows_out, key_out,
    mem, wq, wk, wv, wo, ws, wms, wmo, wmt, wme, edges, win, whid,
    picks, nbrs, dts, serve, pk, r1, tab, acc, tcol, te, sp, sr1, sp2, st, mb, mr1, mp2, mu, selfs, qm, ebase, att, emb, hits, lines, keyline, ghs, slotrows, tk, tv,
    ev, nbt, nslot, sslot, sself, srows, freq, phase,
    in_sem, wl, wsd, wrc, s1s, s1r, s2s, s2r, sbs, sbr, selfsem, backsem, tailsem,
):
    me = lax.axis_index("nodes")
    c = lax.axis_index("mp")
    x, y, z = me // (Y * Z), (me // Z) % Y, me % Z
    p = me // Z
    sib = (me, 1 - c)

    def plane(k, sign):
        dx, dy = k // Y, k % Y
        return ((x + X + sign * dx) % X) * Y + (y + Y + sign * dy) % Y

    def to(g):
        return plane(PLANE - 1 - g, 1 - 2 * c)

    def frm(g, core):
        return plane(PLANE - 1 - g, 2 * core - 1)

    def zpeer(dz):
        return (z + dz) % Z

    def zdev(dz):
        return (p * Z + zpeer(dz), c)

    def remote(src, dst, s, r, dev):
        return pltpu.make_async_remote_copy(src, dst, s, r, device_id=dev, device_id_type=MESH)

    def wait(ref, sem):
        pltpu.make_async_copy(ref, ref, sem).wait()

    mem_cp = pltpu.make_async_copy(memory, mem, in_sem.at[0])
    small = [
        pltpu.make_async_copy(src, dst, in_sem.at[3 + n])
        for n, (src, dst) in enumerate(
            [(sself_h, sself), (srows_h, srows), (ev_h, ev), (nbt_h, nbt), (nslot_h, nslot), (sslot_h, sslot),
             (freq_h, freq), (phase_h, phase)]
        )
    ]
    cols = pl.ds(pl.multiple_of(c * HALF, HALF), HALF)
    rows256 = pl.ds(pl.multiple_of(c * HALF, HALF), HALF)
    rows64 = pl.ds(pl.multiple_of(c * 64, 64), 64)
    shared = [
        (wms_h, wms.at[rows256]), (wmo_h, wmo.at[rows256]), (wmt_h, wmt.at[rows64]), (wme_h, wme.at[rows64]),
        (edge, edges.at[c]), (wq_h, wq.at[:, cols]), (ws_h, ws.at[rows256]), (wk_h, wk.at[:, cols]),
        (wv_h, wv.at[:, cols]), (wo_h, wo.at[rows256]),
    ]
    win_cp = pltpu.make_async_copy(win_h, win, in_sem.at[1])
    whid_cp = pltpu.make_async_copy(whid_h, whid, in_sem.at[2])

    bar = pltpu.get_barrier_semaphore()
    pl.semaphore_signal(bar, inc=1, device_id=sib, device_id_type=MESH)
    for dz in DZ_ORDER:
        pl.semaphore_signal(bar, inc=1, device_id=zdev(dz), device_id_type=MESH)

    def greet(k, _):
        pl.semaphore_signal(bar, inc=1, device_id=(plane(k, 1) * Z + z, c), device_id_type=MESH)
        return 0

    lax.fori_loop(1, PLANE, greet, 0)
    for cp in small[0:2] + [mem_cp] + small[2:]:
        cp.start()
    for n, (src, dst) in enumerate(shared):
        pltpu.make_async_copy(src, dst, wl.at[n]).start()
    win_cp.start()
    whid_cp.start()

    def turn(rows):
        full = jnp.concatenate([rows, jnp.zeros((128 - rows.shape[0], 128), jnp.int32)], axis=0)
        return jnp.transpose(full.astype(F32))

    def spread(block, first):
        n = block.shape[0] * 16
        many = jnp.broadcast_to(block[:, None, :], (block.shape[0], 16, 128)).reshape(n, 128)
        take = iota((n, 128), 1) == first + iota((n, 128), 0) % 16
        return jnp.sum(jnp.where(take, many, 0.0), axis=1, keepdims=True)

    def column(line):
        return jnp.transpose(jnp.broadcast_to(line.astype(F32), (128, 128)))

    lanes2048 = iota((1, ROWS), 1).astype(F32)

    def pick(col):
        return dot(onehot(col == lanes2048), mem[...]).astype(BF16)

    for cp in small:
        cp.wait()
    picks[...] = turn(srows[...])
    by_node = turn(sself[...])
    high = jnp.floor(by_node * 0.0625)
    parts = jnp.concatenate([high, by_node - 16.0 * high], axis=1).astype(BF16)
    si, sj = iota((256, 128), 0), iota((256, 128), 1)
    node = ((si // 2) % PLANE) * Z + si // 32
    both = dot(onehot(sj == node), parts)
    both = 16.0 * both[:, 0:128] + both[:, 128:256]
    for core in range(2):
        col = jnp.sum(jnp.where(sj == 2 * core + si % 2, both, 0.0), axis=1, keepdims=True)
        wide = jnp.broadcast_to(col, (256, 128))
        serve[core] = wide
        for n in range(2):
            lines[pl.ds(2 * core + n, 1), :] = jnp.transpose(wide[128 * n : 128 * n + 128])[0:1]
    mem_cp.wait()

    def pick_self(core, _):
        sp[core] = pick(serve[core, :, pl.ds(0, 1)])
        return 0

    pick_self(c, 0)
    own32 = pl.ds(pl.multiple_of(z * 32, 32), 32)
    own16 = pl.ds(pl.multiple_of(z * 16, 16), 16)
    plane16 = pl.ds(pl.multiple_of(p * 16, 16), 16)
    sr1[own32, :] = sp[c, own32, :]
    pl.semaphore_wait(bar, Z - 1 + PLANE - 1 + 1)
    for dz in DZ_ORDER:
        blk = pl.ds(pl.multiple_of(zpeer(dz) * 32, 32), 32)
        remote(sp.at[c, blk], sr1.at[own32], selfsem.at[0], selfsem.at[1], zdev(dz)).start()
    for n, (src, dst) in enumerate(shared):
        remote(src, dst, wsd.at[n], wrc.at[n], sib).start()

    def step_a(j):
        rows = [picks[pl.ds(pl.multiple_of(to(2 * j + n) * Z, Z), Z), :] for n in range(2)]
        got = pick(spread(jnp.concatenate(rows, axis=0), 16 * c))
        for n in range(2):
            g = 2 * j + n
            pk[g] = got[128 * n : 128 * n + 128]
        for n in range(2):
            g = 2 * j + n
            r1[g, own16, :] = pk[g, own16, :]
            for dz in DZ_ORDER:
                blk = pl.ds(pl.multiple_of(zpeer(dz) * 16, 16), 16)
                remote(pk.at[g, blk], r1.at[g, own16], s1s.at[g], s1r.at[g], zdev(dz)).start()

    def step_b(g):
        wait(r1.at[g, pl.ds(0, 112)], s1r.at[g])

        @pl.when(g < PLANE - 1)
        def _():
            remote(r1.at[g], tab.at[c, p], s2s.at[g], s2r.at[g], (to(g) * Z + z, c)).start()

        @pl.when(g == PLANE - 1)
        def _():
            remote(r1.at[g], tab.at[c, p], sbs.at[g], sbr.at[g], sib).start()
            pltpu.make_async_copy(r1.at[g], tab.at[c, p], s2r.at[g]).start()

    def step_c(g):
        part = tab.at[c, frm(g, c)]
        wait(part, s2r.at[g])

        @pl.when(g < PLANE - 1)
        def _():
            remote(part, part, sbs.at[g], sbr.at[g], sib).start()

    lanes128 = iota((1, 128), 1).astype(F32)

    def step_d(j):
        tables, marks = [], []
        for n in range(2):
            g = 2 * j + n
            wait(tab.at[1 - c, frm(g, 1 - c)], sbr.at[g])
        for n in range(2):
            for core in range(2):
                src = frm(2 * j + n, core)
                tables.append(tab[core, src])
                marks.append(lanes128 + (src * 128 + core * ROWS).astype(F32))
        table = jnp.concatenate(tables, axis=0)

        def tile(m, _):
            r = pl.ds(pl.multiple_of(m * 512, 512), 512)
            at = tcol[r, :]
            oh = jnp.concatenate([onehot(at == mark) for mark in marks], axis=1)
            acc[r, :] = acc[r, :] + dot(oh, table).astype(BF16)
            return 0

        lax.fori_loop(0, 4, tile, 0)

    def first(g, _):
        step_a(g)
        return 0

    lax.fori_loop(0, AHEAD // 2, first, 0)
    pick_self(1 - c, 0)

    slot = nslot[c]
    nbrs[...] = turn((slot % 32 // 16) * ROWS + (slot // 32) * 16 + slot % 16)
    dts[...] = turn(ev[...] - nbt[c])

    def prepare(b, _):
        r = pl.ds(pl.multiple_of(b * 256, 256), 256)
        e = pl.ds(pl.multiple_of(b * 16, 16), 16)
        tcol[r, :] = jnp.broadcast_to(spread(nbrs[e, :], 0), (256, 128))
        te[r, :] = cosine(spread(dts[e, :], 0) * freq[...] + phase[...]).astype(BF16)
        acc[r, :] = jnp.zeros((256, W), BF16)
        return 0

    lax.fori_loop(0, 8, prepare, 0)

    wait(sr1.at[pl.ds(0, 224)], selfsem.at[1])
    out_i, in_j = iota((256, 256), 0), iota((256, 256), 1)
    to_plane = onehot(in_j == ((out_i // 2) % Z) * 32 + (out_i // 16) * 2 + out_i % 2)
    sp2[...] = dot(to_plane, sr1[...]).astype(BF16)
    st[c, plane16, :] = sp2[plane16, :]

    def self_plane(k, _):
        q = plane(k, 1)
        blk = pl.ds(pl.multiple_of(q * 16, 16), 16)
        remote(sp2.at[blk], st.at[c, plane16], selfsem.at[2], selfsem.at[3], (q * Z + z, c)).start()
        return 0

    lax.fori_loop(1, PLANE, self_plane, 0)
    whid_cp.wait()

    def hidden(n, _):
        for g in range(3):
            ghs[g, pl.ds(pl.multiple_of(n * 256, 256), 256), :] = dot(sp[n], whid[g])
        return 0

    lax.fori_loop(0, 2, hidden, 0)

    def do_self():
        wait(st.at[c, pl.ds(0, 240)], selfsem.at[3])
        remote(st.at[c], st.at[c], selfsem.at[4], selfsem.at[5], sib).start()
        for n, (src, dst) in enumerate(shared):
            pltpu.make_async_copy(src, dst, wl.at[n]).wait()
            remote(src, dst, wsd.at[n], wrc.at[n], sib).wait()
        wait(st.at[1 - c], selfsem.at[5])
        table = jnp.concatenate([st[0], st[1]], axis=0)
        lanes512 = iota((128, W), 1).astype(F32)

        ends = (sslot[...] % 4 // 2) * 256 + (sslot[...] // 4) * 2 + sslot[...] % 2
        for n in range(2):
            at = jnp.tile(column(ends[n : n + 1]), (1, 4))
            selfs[pl.ds(128 * n, 128), :] = dot(onehot(at == lanes512), table).astype(BF16)
        mine = selfs[...]
        other = jnp.concatenate([mine[128:256], mine[0:128]], axis=0)
        te_m = jnp.concatenate(
            [cosine(column(ev[...] - nbt[n, 0:1]) * freq[...] + phase[...]).astype(BF16) for n in range(2)], axis=0
        )
        msg = dot(mine, wms[...]) + dot(other, wmo[...]) + dot(te_m, wmt[...])
        feats = jnp.concatenate([edges[0], edges[1]], axis=0)
        shared_part = lax.dot_general(feats, wme[...], (((0,), (0,)), ((), ())), preferred_element_type=F32)
        msg = msg + jnp.concatenate([shared_part, shared_part], axis=0)
        slots = jnp.concatenate([ends[0:1], ends[1:2]], axis=1)
        member = onehot(jnp.broadcast_to(slots, (256, 256)) == out_i + c * 256)
        high = msg.astype(BF16)
        low = (msg - high.astype(F32)).astype(BF16)
        mb[:, pl.ds(0, W)] = (dot(member, high) + dot(member, low)).astype(BF16)
        mb[:, pl.ds(W, 128)] = dot(member, jnp.ones((256, 128), BF16)).astype(BF16)
        mr1[plane16, :] = mb[plane16, :]

        def back_plane(k, _):
            q = plane(k, 1)
            blk = pl.ds(pl.multiple_of(q * 16, 16), 16)
            remote(mb.at[blk], mr1.at[plane16], backsem.at[0], backsem.at[1], (q * Z + z, c)).start()
            return 0

        lax.fori_loop(1, PLANE, back_plane, 0)
        ours = selfs[pl.ds(pl.multiple_of(c * 128, 128), 128), :]
        te_s = jnp.broadcast_to(cosine(phase[...]).astype(BF16), (8, 128))
        query = (dot(ours, wq[pl.ds(0, W), :]) + dot(te_s, wq[pl.ds(W, 128), :])[0:1]).astype(BF16)
        ebase[...] = dot(ours, ws[...])
        head = iota((16, W), 1) // (W // HEADS)
        for t in range(8):
            part = query[16 * t : 16 * t + 16]
            for h in range(HEADS):
                qm[t, pl.ds(16 * h, 16), :] = jnp.where(head == h, part, jnp.zeros_like(part))

    def do_back():
        wait(mr1.at[pl.ds(0, 240)], backsem.at[1])
        to_z = onehot(in_j == ((out_i // 2) % PLANE) * 16 + (out_i // 32) * 2 + out_i % 2)
        mp2[...] = dot(to_z, mr1[...]).astype(BF16)
        mu[c, own32, :] = mp2[own32, :]
        for dz in DZ_ORDER:
            blk = pl.ds(pl.multiple_of(zpeer(dz) * 32, 32), 32)
            remote(mp2.at[blk], mu.at[c, own32], backsem.at[2], backsem.at[3], zdev(dz)).start()

    def do_marks():
        win_cp.wait()
        line = jnp.concatenate([lines[pl.ds(n, 1), :] for n in range(4)], axis=1)
        col = jnp.concatenate([serve[0], serve[1]], axis=0)
        same = jnp.tile(col, (1, 4)) == line
        hits[...] = onehot(same)
        before = same & (iota((512, 512), 0) < iota((512, 512), 1))
        rank = jnp.sum(jnp.where(before, 1.0, 0.0), axis=0, keepdims=True)
        keyline[...] = jnp.where(rank == 0.0, line, -1.0)

    def share_messages():
        wait(mu.at[c, pl.ds(0, 224)], backsem.at[3])
        remote(mu.at[c], mu.at[c], backsem.at[4], backsem.at[5], sib).start()

    def do_share():
        wait(mu.at[1 - c], backsem.at[5])

        def update(n, _):
            r = pl.ds(pl.multiple_of(n * 256, 256), 256)
            sums = dot(hits[r, :], jnp.concatenate([mu[0], mu[1]], axis=0))
            count = sums[:, W : W + 128]
            most = jnp.maximum(count, 1.0)
            mean = jnp.concatenate([sums[:, 128 * k : 128 * k + 128] / most for k in range(4)], axis=1).astype(BF16)
            gi = [dot(mean, win[g]) for g in range(3)]
            gh = [ghs[g, r, :] for g in range(3)]
            reset = jax.nn.sigmoid(gi[0] + gh[0])
            gate = jax.nn.sigmoid(gi[1] + gh[1])
            cand = jnp.tanh(gi[2] + reset * gh[2])
            old = sp[n, :, cols].astype(F32)
            new = (1.0 - gate) * cand + gate * old
            some = jnp.concatenate([count, count], axis=1) > 0
            slotrows[r, :] = jnp.where(some, new, old).astype(BF16)
            return 0

        lax.fori_loop(0, 2, update, 0)

    def tick(i, _):
        @pl.when(i < PLANE)
        def _():
            step_b(i)

        @pl.when((i + AHEAD < PLANE) & (i % 2 == 0))
        def _():
            step_a((i + AHEAD) // 2)

        @pl.when(i == TICK_SELF)
        def _():
            do_self()

        @pl.when(i == TICK_BACK)
        def _():
            do_back()

        @pl.when(i == TICK_MARKS)
        def _():
            do_marks()

            def times(t, _):
                r = pl.ds(pl.multiple_of(t * 512, 512), 512)
                tk[r, :] = dot(te[r, :], wk[pl.ds(W, 128), :])
                tv[r, :] = dot(te[r, :], wv[pl.ds(W, 128), :])
                return 0

            lax.fori_loop(0, 4, times, 0)

        @pl.when((i >= LAG_C) & (i < PLANE + LAG_C))
        def _():
            step_c(i - LAG_C)

        @pl.when((i > LAG_D) & ((i - LAG_D) % 2 == 1))
        def _():
            step_d((i - LAG_D - 1) // 2)

        return 0

    lax.fori_loop(0, TICKS, tick, 0)

    same = (iota((128, 256), 0) % 16) == (iota((128, 256), 1) // 16)
    headcol = iota((16, W), 1) // (W // HEADS)

    def attend(t, _):
        r = pl.ds(pl.multiple_of(t * 512, 512), 512)
        nb = acc[r, :]
        keys = (dot(nb, wk[pl.ds(0, W), :]) + tk[r, :]).astype(BF16)
        vals = (dot(nb, wv[pl.ds(0, W), :]) + tv[r, :]).astype(BF16)

        @pl.when(t == 2)
        def _():
            share_messages()

        for u in range(2):
            k = keys[256 * u : 256 * u + 256]
            score = lax.dot_general(qm[2 * t + u], k, (((1,), (1,)), ((), ())), preferred_element_type=F32) * 0.125
            expo = jnp.where(same, jnp.exp(score), 0.0)
            weights = (expo / jnp.sum(expo, axis=1, keepdims=True)).astype(BF16)
            full = dot(weights, vals[256 * u : 256 * u + 256])
            out = jnp.zeros((16, W), F32)
            for h in range(HEADS):
                out = jnp.where(headcol == h, full[16 * h : 16 * h + 16], out)
            att[pl.ds(pl.multiple_of(t * 32 + 16 * u, 16), 16), :] = out.astype(BF16)
        return 0

    lax.fori_loop(0, 4, attend, 0)
    mine128 = pl.ds(pl.multiple_of(c * 128, 128), 128)
    emb[mine128, :] = (dot(att[...], wo[...]) + ebase[...]).astype(BF16)
    send = remote(emb.at[mine128], emb.at[mine128], tailsem.at[0], tailsem.at[1], sib)
    send.start()
    do_share()
    rows_cp = pltpu.make_async_copy(slotrows, rows_out, tailsem.at[2])
    rows_cp.start()
    key_cp = pltpu.make_async_copy(keyline, key_out, tailsem.at[4])
    key_cp.start()

    def drain(g, _):
        wait(pk.at[g, pl.ds(0, 112)], s1s.at[g])

        @pl.when(g < PLANE - 1)
        def _():
            wait(r1.at[g], s2s.at[g])

        wait(r1.at[g], sbs.at[g])
        return 0

    lax.fori_loop(0, PLANE, drain, 0)
    wait(sp.at[c, pl.ds(0, 224)], selfsem.at[0])
    wait(sp2.at[pl.ds(0, 240)], selfsem.at[2])
    wait(st.at[c], selfsem.at[4])
    wait(mb.at[pl.ds(0, 240)], backsem.at[0])
    wait(mp2.at[pl.ds(0, 224)], backsem.at[2])
    wait(mu.at[c], backsem.at[4])
    send.wait()
    emb_cp = pltpu.make_async_copy(emb, emb_out, tailsem.at[3])
    emb_cp.start()
    rows_cp.wait()
    key_cp.wait()
    emb_cp.wait()


def deliver(emb, rows, key, memory, emb_out, mem_out, ebuf, epair, rbuf, kbuf, old, new, load, store):
    c = lax.axis_index("mp")
    cols = pl.ds(pl.multiple_of(c * HALF, HALF), HALF)
    tiles = [pl.ds(512 * n, 512) for n in range(4)]
    olds = [pltpu.make_async_copy(memory.at[r, cols], old.at[r], load.at[n]) for n, r in enumerate(tiles)]
    news = [pltpu.make_async_copy(new.at[r], mem_out.at[r], store.at[n]) for n, r in enumerate(tiles)]
    rest = [
        pltpu.make_async_copy(key, kbuf, load.at[4]),
        pltpu.make_async_copy(rows, rbuf, load.at[5]),
        pltpu.make_async_copy(emb, ebuf, load.at[6]),
    ]
    for cp in rest + olds:
        cp.start()
    for cp in rest:
        cp.wait()
    for n, r in enumerate(tiles):
        mask = kbuf[...] == (iota((512, 512), 0) + 512 * n).astype(F32)
        hit = jnp.sum(jnp.where(mask, 1.0, 0.0), axis=1, keepdims=True)
        put = dot(onehot(mask), rbuf[...])
        olds[n].wait()
        new[r, :] = jnp.where(hit > 0, put, old[r, :].astype(F32)).astype(BF16)
        news[n].start()
    for n in range(2):
        epair[:, n, :] = ebuf[pl.ds(128 * n, 128), :]
    last = pltpu.make_async_copy(epair, emb_out, store.at[4])
    last.start()
    for cp in news:
        cp.wait()
    last.wait()


def per_device(
    memory, ev_time, nbr_time, edge_feat, self_slot, nbr_slot, serve_self, serve_rows, freq, phase,
    w_query, w_key, w_value, w_out, w_self, w_msg_self, w_msg_other, w_msg_time, w_msg_edge, w_in, w_hid,
):
    hbm = pl.BlockSpec(memory_space=pl.ANY)
    v = lambda *s: pltpu.VMEM(s, BF16)
    vf = lambda *s: pltpu.VMEM(s, F32)
    vi = lambda *s: pltpu.VMEM(s, jnp.int32)
    dma = lambda n: pltpu.SemaphoreType.DMA((n,))
    emb, rows, key = pl.pallas_call(
        kernel,
        out_shape=(
            jax.ShapeDtypeStruct((256, W), BF16), jax.ShapeDtypeStruct((512, HALF), BF16),
            jax.ShapeDtypeStruct((1, 512), F32),
        ),
        in_specs=[hbm] * 21,
        out_specs=(hbm, hbm, hbm),
        scratch_shapes=[
            v(ROWS, W), v(640, W), v(640, W), v(640, W), v(W, W), v(W, W), v(W, W), v(W, W), v(128, W), v(128, W),
            v(2, 64, 128), v(3, W, HALF), v(3, W, HALF),
            vf(128, 128), vf(128, 128), vf(128, 128), vf(2, 256, 128),
            v(16, 128, W), v(16, 128, W), v(2, 16, 128, W), v(2048, W), vf(2048, 128), v(2048, 128),
            v(2, 256, W), v(256, W), v(256, W), v(2, 256, W), v(256, MSGW), v(256, MSGW), v(256, MSGW), v(2, 256, MSGW),
            v(256, W), v(8, 128, W), vf(128, W), v(128, W), v(256, W), v(W, W), vf(4, 128), vf(1, 512), vf(3, 512, HALF), v(512, HALF), vf(2048, W), vf(2048, W),
            vi(1, 128), vi(2, 16, 128), vi(2, 16, 128), vi(2, 128), vi(4, 128), vi(32, 128), vf(1, 128), vf(1, 128),
            dma(11), dma(10), dma(10), dma(10), dma(16), dma(16), dma(16), dma(16), dma(16), dma(16),
            dma(6), dma(6), dma(5),
        ],
        compiler_params=pltpu.CompilerParams(
            collective_id=0, has_side_effects=True, vmem_limit_bytes=60 * 1024 * 1024
        ),
    )(
        ev_time.reshape(1, 128), nbr_time.transpose(1, 2, 0), nbr_slot.transpose(1, 2, 0), self_slot.T,
        serve_self[0].T, serve_rows[0].T, freq.reshape(1, 128), phase.reshape(1, 128), memory, edge_feat.T,
        w_query, w_key, w_value, w_out, w_self,
        w_msg_self, w_msg_other, w_msg_time, w_msg_edge, w_in.transpose(1, 0, 2), w_hid.transpose(1, 0, 2),
    )
    return pl.pallas_call(
        deliver,
        out_shape=(jax.ShapeDtypeStruct((128, 2, W), BF16), jax.ShapeDtypeStruct((ROWS, HALF), BF16)),
        in_specs=[hbm] * 4,
        out_specs=(hbm, hbm),
        scratch_shapes=[
            v(256, W), v(128, 2, W), v(512, HALF), vf(1, 512), v(ROWS, HALF), v(ROWS, HALF), dma(7), dma(5),
        ],
    )(emb, rows, key, memory)


def solution(mesh):
    return jax.shard_map(
        per_device,
        mesh=mesh,
        in_specs=(
            P("nodes", None), P("nodes"), P("nodes", None, None), P("nodes", "mp"), P("nodes", None),
            P("nodes", None, None), P("nodes", None, None), P("nodes", None, None), P(), P(),
            P(None, "mp"), P(None, "mp"), P(None, "mp"), P("mp", None), P("mp", None), P("mp", None),
            P("mp", None), P("mp", None), P("mp", None), P(None, None, "mp"), P(None, None, "mp"),
        ),
        out_specs=(P("nodes", None, None), P("nodes", "mp")),
        check_vma=False,
    )
```

```python
import functools

import jax
import jax.numpy as jnp
from jax import lax
from jax.experimental import pallas as pl
from jax.experimental.pallas import tpu as pltpu
from jax.sharding import PartitionSpec as P

MESH = pl.DeviceIdType.MESH
F32 = jnp.float32
BF16 = jnp.bfloat16
HEADS = 8
X, Y, Z = 4, 4, 8
PLANE = X * Y
W = 512
ROWS = 2048
HALF = W // 2
MSGW = W + 128
DZ_ORDER = (4, 3, 5, 2, 6, 1, 7)
AHEAD = 4
LAG_C, LAG_D = 2, 3
TICKS = PLANE + LAG_D
TICK_SELF, TICK_MARKS, TICK_BACK = 2, 8, 13


def dot(a, b):
    return jnp.dot(a, b, preferred_element_type=F32)


def iota(shape, dim):
    return lax.broadcasted_iota(jnp.int32, shape, dim)


def onehot(mask):
    return jnp.where(mask, 1.0, 0.0).astype(BF16)


def cosine(angle):
    turns = jnp.floor(angle * 0.15915494309189535 + 0.5)
    r = angle - turns * 6.28125
    r = r - turns * 0.0019353071795864769
    h = 0.5 * r
    s = h * h
    poly = 1.6059043836821613e-10
    for coef in (
        -2.5052108385441720e-08,
        2.7557319223985893e-06,
        -1.9841269841269841e-04,
        8.3333333333333333e-03,
        -1.6666666666666666e-01,
        1.0,
    ):
        poly = poly * s + coef
    sine = poly * h
    return 1.0 - 2.0 * sine * sine


def kernel(
    ev_h, nbt_h, nslot_h, sslot_h, sself_h, srows_h, freq_h, phase_h, memory, edge, wq_h, wk_h, wv_h, wo_h, ws_h, wms_h, wmo_h, wmt_h, wme_h, win_h, whid_h,
    emb_out, rows_out, key_out,
    mem, wq, wk, wv, wo, ws, wms, wmo, wmt, wme, edges, win, whid,
    picks, nbrs, dts, serve, pk, r1, tab, acc, tcol, te, sp, sr1, sp2, st, mb, mr1, mp2, mu, selfs, qm, ebase, att, emb, hits, lines, keyline, ghs, slotrows, tk, tv,
    ev, nbt, nslot, sslot, sself, srows, freq, phase,
    in_sem, wl, wsd, wrc, s1s, s1r, s2s, s2r, sbs, sbr, selfsem, backsem, tailsem,
):
    me = lax.axis_index("nodes")
    c = lax.axis_index("mp")
    x, y, z = me // (Y * Z), (me // Z) % Y, me % Z
    p = me // Z
    sib = (me, 1 - c)

    def plane(k, sign):
        dx, dy = k // Y, k % Y
        return ((x + X + sign * dx) % X) * Y + (y + Y + sign * dy) % Y

    def to(g):
        return plane(PLANE - 1 - g, 1 - 2 * c)

    def frm(g, core):
        return plane(PLANE - 1 - g, 2 * core - 1)

    def zpeer(dz):
        return (z + dz) % Z

    def zdev(dz):
        return (p * Z + zpeer(dz), c)

    def remote(src, dst, s, r, dev):
        return pltpu.make_async_remote_copy(src, dst, s, r, device_id=dev, device_id_type=MESH)

    def wait(ref, sem):
        pltpu.make_async_copy(ref, ref, sem).wait()

    mem_cp = pltpu.make_async_copy(memory, mem, in_sem.at[0])
    small = [
        pltpu.make_async_copy(src, dst, in_sem.at[3 + n])
        for n, (src, dst) in enumerate(
            [(sself_h, sself), (srows_h, srows), (ev_h, ev), (nbt_h, nbt), (nslot_h, nslot), (sslot_h, sslot),
             (freq_h, freq), (phase_h, phase)]
        )
    ]
    cols = pl.ds(pl.multiple_of(c * HALF, HALF), HALF)
    rows256 = pl.ds(pl.multiple_of(c * HALF, HALF), HALF)
    rows64 = pl.ds(pl.multiple_of(c * 64, 64), 64)
    shared = [
        (wms_h, wms.at[rows256]), (wmo_h, wmo.at[rows256]), (wmt_h, wmt.at[rows64]), (wme_h, wme.at[rows64]),
        (edge, edges.at[c]), (wq_h, wq.at[:, cols]), (ws_h, ws.at[rows256]), (wk_h, wk.at[:, cols]),
        (wv_h, wv.at[:, cols]), (wo_h, wo.at[rows256]),
    ]
    win_cp = pltpu.make_async_copy(win_h, win, in_sem.at[1])
    whid_cp = pltpu.make_async_copy(whid_h, whid, in_sem.at[2])

    bar = pltpu.get_barrier_semaphore()
    pl.semaphore_signal(bar, inc=1, device_id=sib, device_id_type=MESH)
    for dz in DZ_ORDER:
        pl.semaphore_signal(bar, inc=1, device_id=zdev(dz), device_id_type=MESH)

    def greet(k, _):
        pl.semaphore_signal(bar, inc=1, device_id=(plane(k, 1) * Z + z, c), device_id_type=MESH)
        return 0

    lax.fori_loop(1, PLANE, greet, 0)
    for cp in small[0:2] + [mem_cp] + small[2:]:
        cp.start()
    for n, (src, dst) in enumerate(shared):
        pltpu.make_async_copy(src, dst, wl.at[n]).start()
    win_cp.start()
    whid_cp.start()

    def turn(rows):
        full = jnp.concatenate([rows, jnp.zeros((128 - rows.shape[0], 128), jnp.int32)], axis=0)
        return jnp.transpose(full.astype(F32))

    def spread(block, first):
        n = block.shape[0] * 16
        many = jnp.broadcast_to(block[:, None, :], (block.shape[0], 16, 128)).reshape(n, 128)
        take = iota((n, 128), 1) == first + iota((n, 128), 0) % 16
        return jnp.sum(jnp.where(take, many, 0.0), axis=1, keepdims=True)

    def column(line):
        return jnp.transpose(jnp.broadcast_to(line.astype(F32), (128, 128)))

    lanes2048 = iota((1, ROWS), 1).astype(F32)

    def pick(col):
        return dot(onehot(col == lanes2048), mem[...]).astype(BF16)

    for cp in small:
        cp.wait()
    picks[...] = turn(srows[...])
    by_node = turn(sself[...])
    high = jnp.floor(by_node * 0.0625)
    parts = jnp.concatenate([high, by_node - 16.0 * high], axis=1).astype(BF16)
    si, sj = iota((256, 128), 0), iota((256, 128), 1)
    node = ((si // 2) % PLANE) * Z + si // 32
    both = dot(onehot(sj == node), parts)
    both = 16.0 * both[:, 0:128] + both[:, 128:256]
    for core in range(2):
        col = jnp.sum(jnp.where(sj == 2 * core + si % 2, both, 0.0), axis=1, keepdims=True)
        wide = jnp.broadcast_to(col, (256, 128))
        serve[core] = wide
        for n in range(2):
            lines[pl.ds(2 * core + n, 1), :] = jnp.transpose(wide[128 * n : 128 * n + 128])[0:1]
    mem_cp.wait()

    def pick_self(core, _):
        sp[core] = pick(serve[core, :, pl.ds(0, 1)])
        return 0

    pick_self(c, 0)
    own32 = pl.ds(pl.multiple_of(z * 32, 32), 32)
    own16 = pl.ds(pl.multiple_of(z * 16, 16), 16)
    plane16 = pl.ds(pl.multiple_of(p * 16, 16), 16)
    sr1[own32, :] = sp[c, own32, :]
    pl.semaphore_wait(bar, Z - 1 + PLANE - 1 + 1)
    for dz in DZ_ORDER:
        blk = pl.ds(pl.multiple_of(zpeer(dz) * 32, 32), 32)
        remote(sp.at[c, blk], sr1.at[own32], selfsem.at[0], selfsem.at[1], zdev(dz)).start()
    for n, (src, dst) in enumerate(shared):
        remote(src, dst, wsd.at[n], wrc.at[n], sib).start()

    def step_a(j):
        rows = [picks[pl.ds(pl.multiple_of(to(2 * j + n) * Z, Z), Z), :] for n in range(2)]
        got = pick(spread(jnp.concatenate(rows, axis=0), 16 * c))
        for n in range(2):
            g = 2 * j + n
            pk[g] = got[128 * n : 128 * n + 128]
        for n in range(2):
            g = 2 * j + n
            r1[g, own16, :] = pk[g, own16, :]
            for dz in DZ_ORDER:
                blk = pl.ds(pl.multiple_of(zpeer(dz) * 16, 16), 16)
                remote(pk.at[g, blk], r1.at[g, own16], s1s.at[g], s1r.at[g], zdev(dz)).start()

    def step_b(g):
        wait(r1.at[g, pl.ds(0, 112)], s1r.at[g])

        @pl.when(g < PLANE - 1)
        def _():
            remote(r1.at[g], tab.at[c, p], s2s.at[g], s2r.at[g], (to(g) * Z + z, c)).start()

        @pl.when(g == PLANE - 1)
        def _():
            remote(r1.at[g], tab.at[c, p], sbs.at[g], sbr.at[g], sib).start()
            pltpu.make_async_copy(r1.at[g], tab.at[c, p], s2r.at[g]).start()

    def step_c(g):
        part = tab.at[c, frm(g, c)]
        wait(part, s2r.at[g])

        @pl.when(g < PLANE - 1)
        def _():
            remote(part, part, sbs.at[g], sbr.at[g], sib).start()

    lanes128 = iota((1, 128), 1).astype(F32)

    def step_d(j):
        tables, marks = [], []
        for n in range(2):
            g = 2 * j + n
            wait(tab.at[1 - c, frm(g, 1 - c)], sbr.at[g])
        for n in range(2):
            for core in range(2):
                src = frm(2 * j + n, core)
                tables.append(tab[core, src])
                marks.append(lanes128 + (src * 128 + core * ROWS).astype(F32))
        table = jnp.concatenate(tables, axis=0)

        def tile(m, _):
            r = pl.ds(pl.multiple_of(m * 512, 512), 512)
            at = tcol[r, :]
            oh = jnp.concatenate([onehot(at == mark) for mark in marks], axis=1)
            acc[r, :] = acc[r, :] + dot(oh, table).astype(BF16)
            return 0

        lax.fori_loop(0, 4, tile, 0)

    def first(g, _):
        step_a(g)
        return 0

    lax.fori_loop(0, AHEAD // 2, first, 0)
    pick_self(1 - c, 0)

    slot = nslot[c]
    nbrs[...] = turn((slot % 32 // 16) * ROWS + (slot // 32) * 16 + slot % 16)
    dts[...] = turn(ev[...] - nbt[c])

    def prepare(b, _):
        r = pl.ds(pl.multiple_of(b * 256, 256), 256)
        e = pl.ds(pl.multiple_of(b * 16, 16), 16)
        tcol[r, :] = jnp.broadcast_to(spread(nbrs[e, :], 0), (256, 128))
        te[r, :] = cosine(spread(dts[e, :], 0) * freq[...] + phase[...]).astype(BF16)
        acc[r, :] = jnp.zeros((256, W), BF16)
        return 0

    lax.fori_loop(0, 8, prepare, 0)

    wait(sr1.at[pl.ds(0, 224)], selfsem.at[1])
    out_i, in_j = iota((256, 256), 0), iota((256, 256), 1)
    to_plane = onehot(in_j == ((out_i // 2) % Z) * 32 + (out_i // 16) * 2 + out_i % 2)
    sp2[...] = dot(to_plane, sr1[...]).astype(BF16)
    st[c, plane16, :] = sp2[plane16, :]

    def self_plane(k, _):
        q = plane(k, 1)
        blk = pl.ds(pl.multiple_of(q * 16, 16), 16)
        remote(sp2.at[blk], st.at[c, plane16], selfsem.at[2], selfsem.at[3], (q * Z + z, c)).start()
        return 0

    lax.fori_loop(1, PLANE, self_plane, 0)
    whid_cp.wait()

    def hidden(n, _):
        for g in range(3):
            ghs[g, pl.ds(pl.multiple_of(n * 256, 256), 256), :] = dot(sp[n], whid[g])
        return 0

    lax.fori_loop(0, 2, hidden, 0)

    def do_self():
        wait(st.at[c, pl.ds(0, 240)], selfsem.at[3])
        remote(st.at[c], st.at[c], selfsem.at[4], selfsem.at[5], sib).start()
        for n, (src, dst) in enumerate(shared):
            pltpu.make_async_copy(src, dst, wl.at[n]).wait()
            remote(src, dst, wsd.at[n], wrc.at[n], sib).wait()
        wait(st.at[1 - c], selfsem.at[5])
        table = jnp.concatenate([st[0], st[1]], axis=0)
        lanes512 = iota((128, W), 1).astype(F32)

        ends = (sslot[...] % 4 // 2) * 256 + (sslot[...] // 4) * 2 + sslot[...] % 2
        for n in range(2):
            at = jnp.tile(column(ends[n : n + 1]), (1, 4))
            selfs[pl.ds(128 * n, 128), :] = dot(onehot(at == lanes512), table).astype(BF16)
        mine = selfs[...]
        other = jnp.concatenate([mine[128:256], mine[0:128]], axis=0)
        te_m = jnp.concatenate(
            [cosine(column(ev[...] - nbt[n, 0:1]) * freq[...] + phase[...]).astype(BF16) for n in range(2)], axis=0
        )
        msg = dot(mine, wms[...]) + dot(other, wmo[...]) + dot(te_m, wmt[...])
        feats = jnp.concatenate([edges[0], edges[1]], axis=0)
        shared_part = lax.dot_general(feats, wme[...], (((0,), (0,)), ((), ())), preferred_element_type=F32)
        msg = msg + jnp.concatenate([shared_part, shared_part], axis=0)
        slots = jnp.concatenate([ends[0:1], ends[1:2]], axis=1)
        member = onehot(jnp.broadcast_to(slots, (256, 256)) == out_i + c * 256)
        high = msg.astype(BF16)
        low = (msg - high.astype(F32)).astype(BF16)
        mb[:, pl.ds(0, W)] = (dot(member, high) + dot(member, low)).astype(BF16)
        mb[:, pl.ds(W, 128)] = dot(member, jnp.ones((256, 128), BF16)).astype(BF16)
        mr1[plane16, :] = mb[plane16, :]

        def back_plane(k, _):
            q = plane(k, 1)
            blk = pl.ds(pl.multiple_of(q * 16, 16), 16)
            remote(mb.at[blk], mr1.at[plane16], backsem.at[0], backsem.at[1], (q * Z + z, c)).start()
            return 0

        lax.fori_loop(1, PLANE, back_plane, 0)
        ours = selfs[pl.ds(pl.multiple_of(c * 128, 128), 128), :]
        te_s = jnp.broadcast_to(cosine(phase[...]).astype(BF16), (8, 128))
        query = (dot(ours, wq[pl.ds(0, W), :]) + dot(te_s, wq[pl.ds(W, 128), :])[0:1]).astype(BF16)
        ebase[...] = dot(ours, ws[...])
        head = iota((16, W), 1) // (W // HEADS)
        for t in range(8):
            part = query[16 * t : 16 * t + 16]
            for h in range(HEADS):
                qm[t, pl.ds(16 * h, 16), :] = jnp.where(head == h, part, jnp.zeros_like(part))

    def do_back():
        wait(mr1.at[pl.ds(0, 240)], backsem.at[1])
        to_z = onehot(in_j == ((out_i // 2) % PLANE) * 16 + (out_i // 32) * 2 + out_i % 2)
        mp2[...] = dot(to_z, mr1[...]).astype(BF16)
        mu[c, own32, :] = mp2[own32, :]
        for dz in DZ_ORDER:
            blk = pl.ds(pl.multiple_of(zpeer(dz) * 32, 32), 32)
            remote(mp2.at[blk], mu.at[c, own32], backsem.at[2], backsem.at[3], zdev(dz)).start()

    def do_marks():
        win_cp.wait()
        line = jnp.concatenate([lines[pl.ds(n, 1), :] for n in range(4)], axis=1)
        col = jnp.concatenate([serve[0], serve[1]], axis=0)
        same = jnp.tile(col, (1, 4)) == line
        hits[...] = onehot(same)
        before = same & (iota((512, 512), 0) < iota((512, 512), 1))
        rank = jnp.sum(jnp.where(before, 1.0, 0.0), axis=0, keepdims=True)
        keyline[...] = jnp.where(rank == 0.0, line, -1.0)

    def share_messages():
        wait(mu.at[c, pl.ds(0, 224)], backsem.at[3])
        remote(mu.at[c], mu.at[c], backsem.at[4], backsem.at[5], sib).start()

    def do_share():
        wait(mu.at[1 - c], backsem.at[5])

        def update(n, _):
            r = pl.ds(pl.multiple_of(n * 256, 256), 256)
            sums = dot(hits[r, :], jnp.concatenate([mu[0], mu[1]], axis=0))
            count = sums[:, W : W + 128]
            most = jnp.maximum(count, 1.0)
            mean = jnp.concatenate([sums[:, 128 * k : 128 * k + 128] / most for k in range(4)], axis=1).astype(BF16)
            gi = [dot(mean, win[g]) for g in range(3)]
            gh = [ghs[g, r, :] for g in range(3)]
            reset = jax.nn.sigmoid(gi[0] + gh[0])
            gate = jax.nn.sigmoid(gi[1] + gh[1])
            cand = jnp.tanh(gi[2] + reset * gh[2])
            old = sp[n, :, cols].astype(F32)
            new = (1.0 - gate) * cand + gate * old
            some = jnp.concatenate([count, count], axis=1) > 0
            slotrows[r, :] = jnp.where(some, new, old).astype(BF16)
            return 0

        lax.fori_loop(0, 2, update, 0)

    def tick(i, _):
        @pl.when(i < PLANE)
        def _():
            step_b(i)

        @pl.when((i + AHEAD < PLANE) & (i % 2 == 0))
        def _():
            step_a((i + AHEAD) // 2)

        @pl.when(i == TICK_SELF)
        def _():
            do_self()

        @pl.when(i == TICK_BACK)
        def _():
            do_back()

        @pl.when(i == TICK_MARKS)
        def _():
            do_marks()

            def times(t, _):
                r = pl.ds(pl.multiple_of(t * 512, 512), 512)
                tk[r, :] = dot(te[r, :], wk[pl.ds(W, 128), :])
                tv[r, :] = dot(te[r, :], wv[pl.ds(W, 128), :])
                return 0

            lax.fori_loop(0, 4, times, 0)

        @pl.when((i >= LAG_C) & (i < PLANE + LAG_C))
        def _():
            step_c(i - LAG_C)

        @pl.when((i > LAG_D) & ((i - LAG_D) % 2 == 1))
        def _():
            step_d((i - LAG_D - 1) // 2)

        return 0

    lax.fori_loop(0, TICKS, tick, 0)

    same = (iota((128, 256), 0) % 16) == (iota((128, 256), 1) // 16)
    headcol = iota((16, W), 1) // (W // HEADS)

    def attend(t, _):
        r = pl.ds(pl.multiple_of(t * 512, 512), 512)
        nb = acc[r, :]
        keys = (dot(nb, wk[pl.ds(0, W), :]) + tk[r, :]).astype(BF16)
        vals = (dot(nb, wv[pl.ds(0, W), :]) + tv[r, :]).astype(BF16)

        @pl.when(t == 2)
        def _():
            share_messages()

        for u in range(2):
            k = keys[256 * u : 256 * u + 256]
            score = lax.dot_general(qm[2 * t + u], k, (((1,), (1,)), ((), ())), preferred_element_type=F32) * 0.125
            expo = jnp.where(same, jnp.exp(score), 0.0)
            weights = (expo / jnp.sum(expo, axis=1, keepdims=True)).astype(BF16)
            full = dot(weights, vals[256 * u : 256 * u + 256])
            out = jnp.zeros((16, W), F32)
            for h in range(HEADS):
                out = jnp.where(headcol == h, full[16 * h : 16 * h + 16], out)
            att[pl.ds(pl.multiple_of(t * 32 + 16 * u, 16), 16), :] = out.astype(BF16)
        return 0

    lax.fori_loop(0, 4, attend, 0)
    mine128 = pl.ds(pl.multiple_of(c * 128, 128), 128)
    emb[mine128, :] = (dot(att[...], wo[...]) + ebase[...]).astype(BF16)
    send = remote(emb.at[mine128], emb.at[mine128], tailsem.at[0], tailsem.at[1], sib)
    send.start()
    do_share()
    rows_cp = pltpu.make_async_copy(slotrows, rows_out, tailsem.at[2])
    rows_cp.start()
    key_cp = pltpu.make_async_copy(keyline, key_out, tailsem.at[4])
    key_cp.start()

    def drain(g, _):
        wait(pk.at[g, pl.ds(0, 112)], s1s.at[g])

        @pl.when(g < PLANE - 1)
        def _():
            wait(r1.at[g], s2s.at[g])

        wait(r1.at[g], sbs.at[g])
        return 0

    lax.fori_loop(0, PLANE, drain, 0)
    wait(sp.at[c, pl.ds(0, 224)], selfsem.at[0])
    wait(sp2.at[pl.ds(0, 240)], selfsem.at[2])
    wait(st.at[c], selfsem.at[4])
    wait(mb.at[pl.ds(0, 240)], backsem.at[0])
    wait(mp2.at[pl.ds(0, 224)], backsem.at[2])
    wait(mu.at[c], backsem.at[4])
    send.wait()
    emb_cp = pltpu.make_async_copy(emb, emb_out, tailsem.at[3])
    emb_cp.start()
    rows_cp.wait()
    key_cp.wait()
    emb_cp.wait()


def deliver(emb, rows, key, memory, emb_out, mem_out, ebuf, epair, rbuf, kbuf, old, new, load, store):
    c = lax.axis_index("mp")
    cols = pl.ds(pl.multiple_of(c * HALF, HALF), HALF)
    tiles = [pl.ds(256 * n, 256) for n in range(8)]
    olds = [pltpu.make_async_copy(memory.at[r, cols], old.at[r], load.at[n]) for n, r in enumerate(tiles)]
    news = [pltpu.make_async_copy(new.at[r], mem_out.at[r], store.at[n]) for n, r in enumerate(tiles)]
    rest = [
        pltpu.make_async_copy(key, kbuf, load.at[8]),
        pltpu.make_async_copy(rows, rbuf, load.at[9]),
        pltpu.make_async_copy(emb, ebuf, load.at[10]),
    ]
    for cp in rest + olds:
        cp.start()
    last = pltpu.make_async_copy(epair, emb_out, store.at[8])
    for cp in rest[0:2]:
        cp.wait()
    for n, r in enumerate(tiles):
        mask = kbuf[...] == (iota((256, 512), 0) + 256 * n).astype(F32)
        hit = jnp.sum(jnp.where(mask, 1.0, 0.0), axis=1, keepdims=True)
        put = dot(onehot(mask), rbuf[...])
        olds[n].wait()
        new[r, :] = jnp.where(hit > 0, put, old[r, :].astype(F32)).astype(BF16)
        news[n].start()
        if n == 1:
            rest[2].wait()
            for j in range(2):
                epair[:, j, :] = ebuf[pl.ds(128 * j, 128), :]
        if n == 3:
            last.start()
    for cp in news:
        cp.wait()
    last.wait()


def per_device(
    memory, ev_time, nbr_time, edge_feat, self_slot, nbr_slot, serve_self, serve_rows, freq, phase,
    w_query, w_key, w_value, w_out, w_self, w_msg_self, w_msg_other, w_msg_time, w_msg_edge, w_in, w_hid,
):
    hbm = pl.BlockSpec(memory_space=pl.ANY)
    v = lambda *s: pltpu.VMEM(s, BF16)
    vf = lambda *s: pltpu.VMEM(s, F32)
    vi = lambda *s: pltpu.VMEM(s, jnp.int32)
    dma = lambda n: pltpu.SemaphoreType.DMA((n,))
    emb, rows, key = pl.pallas_call(
        kernel,
        out_shape=(
            jax.ShapeDtypeStruct((256, W), BF16), jax.ShapeDtypeStruct((512, HALF), BF16),
            jax.ShapeDtypeStruct((1, 512), F32),
        ),
        in_specs=[hbm] * 21,
        out_specs=(hbm, hbm, hbm),
        scratch_shapes=[
            v(ROWS, W), v(640, W), v(640, W), v(640, W), v(W, W), v(W, W), v(W, W), v(W, W), v(128, W), v(128, W),
            v(2, 64, 128), v(3, W, HALF), v(3, W, HALF),
            vf(128, 128), vf(128, 128), vf(128, 128), vf(2, 256, 128),
            v(16, 128, W), v(16, 128, W), v(2, 16, 128, W), v(2048, W), vf(2048, 128), v(2048, 128),
            v(2, 256, W), v(256, W), v(256, W), v(2, 256, W), v(256, MSGW), v(256, MSGW), v(256, MSGW), v(2, 256, MSGW),
            v(256, W), v(8, 128, W), vf(128, W), v(128, W), v(256, W), v(W, W), vf(4, 128), vf(1, 512), vf(3, 512, HALF), v(512, HALF), vf(2048, W), vf(2048, W),
            vi(1, 128), vi(2, 16, 128), vi(2, 16, 128), vi(2, 128), vi(4, 128), vi(32, 128), vf(1, 128), vf(1, 128),
            dma(11), dma(10), dma(10), dma(10), dma(16), dma(16), dma(16), dma(16), dma(16), dma(16),
            dma(6), dma(6), dma(5),
        ],
        compiler_params=pltpu.CompilerParams(
            collective_id=0, has_side_effects=True, vmem_limit_bytes=60 * 1024 * 1024
        ),
    )(
        ev_time.reshape(1, 128), nbr_time.transpose(1, 2, 0), nbr_slot.transpose(1, 2, 0), self_slot.T,
        serve_self[0].T, serve_rows[0].T, freq.reshape(1, 128), phase.reshape(1, 128), memory, edge_feat.T,
        w_query, w_key, w_value, w_out, w_self,
        w_msg_self, w_msg_other, w_msg_time, w_msg_edge, w_in.transpose(1, 0, 2), w_hid.transpose(1, 0, 2),
    )
    return pl.pallas_call(
        deliver,
        out_shape=(jax.ShapeDtypeStruct((128, 2, W), BF16), jax.ShapeDtypeStruct((ROWS, HALF), BF16)),
        in_specs=[hbm] * 4,
        out_specs=(hbm, hbm),
        scratch_shapes=[
            v(256, W), v(128, 2, W), v(512, HALF), vf(1, 512), v(ROWS, HALF), v(ROWS, HALF), dma(11), dma(9),
        ],
    )(emb, rows, key, memory)


def solution(mesh):
    return jax.shard_map(
        per_device,
        mesh=mesh,
        in_specs=(
            P("nodes", None), P("nodes"), P("nodes", None, None), P("nodes", "mp"), P("nodes", None),
            P("nodes", None, None), P("nodes", None, None), P("nodes", None, None), P(), P(),
            P(None, "mp"), P(None, "mp"), P(None, "mp"), P("mp", None), P("mp", None), P("mp", None),
            P("mp", None), P("mp", None), P("mp", None), P(None, None, "mp"), P(None, None, "mp"),
        ),
        out_specs=(P("nodes", None, None), P("nodes", "mp")),
        check_vma=False,
    )
```
